128 devices in a mesh: shot: 8 (over y_lo, z), gx: 4 (over x), gy: 4 (over y_hi, core).
Axes of the slice: x: 4, y: 4 (y_hi: 2, y_lo: 2; y = y_hi * 2 + y_lo), z: 4, core: 2. Of those that a mesh axis runs over, the one named last changes fastest.
Arguments:
- stiffness: float32 [192, 64, 256], P('gx', 'gy'), may hold values from 0.03 to 0.1
- buoyancy: float32 [192, 64, 256], P('gx', 'gy'), may hold values from 0.05 to 1.6
- fwd_prev: float32 [8, 192, 64, 256], P('shot', 'gx', 'gy'), may hold values from -6 to 6
- fwd_now: float32 [8, 192, 64, 256], P('shot', 'gx', 'gy'), may hold values from -6 to 6
- adj_prev: float32 [8, 192, 64, 256], P('shot', 'gx', 'gy'), may hold values from -6 to 6
- adj_now: float32 [8, 192, 64, 256], P('shot', 'gx', 'gy'), may hold values from -6 to 6
- wavelet: float32 [8, 4], P('shot'), may hold values from -160 to 160
- source_cell: int32 [8, 3], P('shot'), may hold values from 0 to 255, as said below
- receiver_cell: int32 [8, 512, 3], P('shot'), may hold values from 0 to 255, as said below
- traces: float32 [8, 512, 4], P('shot'), may hold values from -60 to 60
- aperture_blocks: int32 [8, 4, 4, 8, 1], replicated, may hold values from 0 to 2, as said below
- aperture_count: int32 [8, 4, 4, 8], replicated, may hold values from 0 to 1, as said below
Outputs:
- fwd_final: float32 [8, 192, 64, 256], P('shot', 'gx', 'gy')
- adj_final: float32 [8, 192, 64, 256], P('shot', 'gx', 'gy')
- gradient: float32 [4, 24, 32, 128], P('gx', 'shot', 'gy')
The draws below stay inside these ranges and needn't reach their ends.
Inputs may be any that keep to these rules, and one draw needn't show every extreme that they name: `aperture_blocks`: entries of one list are distinct local coarse rows, 0 to 2. `aperture_count`: some list is full and some empty in every draw; slots past the count hold rows that are to be ignored. `source_cell`: each entry is a cell inside the grid: x below 192, y below 64, depth below 256. `receiver_cell`: each entry is a cell inside the grid: x below 192, y below 64, depth below 256; cells may repeat.
All inputs are finite; a program needn't handle non-finite values.
Results may differ from the reference program's by a relative error of at most 0.024.
Values sent between devices are 32-bit elements; how exact they have to be, the bound alone decides.
A program may use at most 128 MiB of HBM per device.

```python
import math
import jax
import jax.numpy as jnp
from jax import lax

STEPS = 4
NREC = 512
SHOTS = 8
NX = 192
NY = 64
NZ = 256
NZC = 128
NXC = 96
NYC = 32
KPO = 3
CAP = 1
N_SHOT = 8
N_GX = 4
N_GY = 4


def draw_source_cell(key, part):
    keys = jax.random.split(jax.random.fold_in(key, 11), 3)
    along_x = jax.random.randint(keys[0], (SHOTS,), 0, NX)
    along_y = jax.random.randint(keys[1], (SHOTS,), 0, NY)
    along_z = jax.random.randint(keys[2], (SHOTS,), 0, NZ)
    along_x = along_x.at[0].set(NX - 1).at[SHOTS - 1].set(0)
    along_y = along_y.at[0].set(NY - 1)
    along_z = along_z.at[0].set(NZ - 1)
    return jnp.stack([along_x, along_y, along_z], axis=1).astype(jnp.int32)


def draw_receiver_cell(key, part):
    keys = jax.random.split(jax.random.fold_in(key, 13), 3)
    along_x = jax.random.randint(keys[0], (SHOTS, NREC), 0, NX)
    along_y = jax.random.randint(keys[1], (SHOTS, NREC), 0, NY)
    along_z = jax.random.randint(keys[2], (SHOTS, NREC), 0, NZ)
    along_x = along_x.at[0, 0].set(0).at[0, 1].set(NX - 1)
    along_y = along_y.at[0, 0].set(0).at[0, 1].set(NY - 1)
    along_z = along_z.at[0, 0].set(0).at[0, 1].set(NZ - 1)
    return jnp.stack([along_x, along_y, along_z], axis=2).astype(jnp.int32)


def draw_aperture_blocks(key, part):
    scores = jax.random.randint(jax.random.fold_in(key, 17), (SHOTS, N_GX, N_GY, N_SHOT, KPO), 0, 2 ** 20)
    scores = scores * KPO + jnp.arange(KPO, dtype=jnp.int32)
    order = jnp.argsort(scores, axis=-1, stable=True)
    return order[..., :CAP].astype(jnp.int32)


def draw_aperture_count(key, part):
    keys = jax.random.split(jax.random.fold_in(key, 19), 3)
    total = SHOTS * N_GX * N_GY * N_SHOT
    counts = jax.random.randint(keys[0], (total,), 0, CAP + 1)
    first = jax.random.randint(keys[1], (), 0, total)
    second = (first + 1 + jax.random.randint(keys[2], (), 0, total - 1)) % total
    counts = counts.at[first].set(CAP).at[second].set(0)
    return counts.reshape(SHOTS, N_GX, N_GY, N_SHOT).astype(jnp.int32)


def level_of(stream_key, shape, cuts, low, high):
    factor_of = 1.0
    for dim, shards_of in cuts:
        draws = jax.random.uniform(jax.random.fold_in(jax.random.fold_in(stream_key, 6), dim), (shards_of,), jnp.float32, low / len(cuts), high / len(cuts))
        factor_of = factor_of * jnp.repeat(jnp.exp(draws), shape[dim] // shards_of).reshape((-1,) + (1,) * (len(shape) - 1 - dim))
    return factor_of


def centred(rng, shape, deviation, limit, cuts=(), kind=jnp.bfloat16):
    entries = jax.random.normal(rng, shape, jnp.float32) * deviation
    if len(cuts) > 0:
        entries = level_of(rng, shape, cuts, -0.22, 0.18) * entries
    return jnp.clip(entries, min=-limit, max=limit).astype(kind)


def setup_inputs(seed: int = 0) -> dict:
    arg_keys = jax.random.split(jax.random.key(seed), 13)
    return {
        "stiffness": jnp.clip(jnp.exp(math.log(0.1) - 1.2039728 * jax.random.uniform(arg_keys[0], (NX, NY, NZ), jnp.float32) ** level_of(arg_keys[0], (NX, NY, NZ), ((0, 4), (1, 4)), -0.2, 0.2)), 0.03, 0.1),
        "buoyancy": jnp.clip(jnp.exp(math.log(1.6) - 3.465736 * jax.random.uniform(arg_keys[1], (NX, NY, NZ), jnp.float32) ** level_of(arg_keys[1], (NX, NY, NZ), ((0, 4), (1, 4)), -0.2, 0.2)), 0.05, 1.6),
        "fwd_prev": centred(arg_keys[2], (SHOTS, NX, NY, NZ), 1.0, 6.0, ((0, 8), (1, 4), (2, 4)), jnp.float32),
        "fwd_now": centred(arg_keys[3], (SHOTS, NX, NY, NZ), 1.0, 6.0, ((0, 8), (1, 4), (2, 4)), jnp.float32),
        "adj_prev": centred(arg_keys[4], (SHOTS, NX, NY, NZ), 1.0, 6.0, ((0, 8), (1, 4), (2, 4)), jnp.float32),
        "adj_now": centred(arg_keys[5], (SHOTS, NX, NY, NZ), 1.0, 6.0, ((0, 8), (1, 4), (2, 4)), jnp.float32),
        "wavelet": centred(arg_keys[6], (SHOTS, STEPS), 20.0, 160.0, ((0, 8),), jnp.float32),
        "source_cell": draw_source_cell(jax.random.fold_in(arg_keys[12], 71), 0),
        "receiver_cell": draw_receiver_cell(jax.random.fold_in(arg_keys[12], 71), 0),
        "traces": centred(arg_keys[9], (SHOTS, NREC, STEPS), 10.0, 60.0, ((0, 8),), jnp.float32),
        "aperture_blocks": draw_aperture_blocks(jax.random.fold_in(arg_keys[12], 71), 0),
        "aperture_count": draw_aperture_count(jax.random.fold_in(arg_keys[12], 71), 0),
    }


second_coef = (-205.0 / 72.0, 8.0 / 5.0, -1.0 / 5.0, 8.0 / 315.0, -1.0 / 560.0)
first_coef = (4.0 / 5.0, -1.0 / 5.0, 4.0 / 105.0, -1.0 / 280.0)


def shifted(extended, along, offset, sizes):
    starts = [4, 4, 4]
    starts[along] = 4 + offset
    return extended[starts[0]:starts[0] + sizes[0], starts[1]:starts[1] + sizes[1], starts[2]:starts[2] + sizes[2]]


def derivatives(padded):
    sizes = (padded.shape[0] - 8, padded.shape[1] - 8, padded.shape[2])
    extended = jnp.pad(padded, ((0, 0), (0, 0), (4, 4)))
    center = shifted(extended, 0, 0, sizes)
    laplace = 3.0 * second_coef[0] * center
    firsts = []
    for along in range(3):
        slope = jnp.zeros(sizes, jnp.float32)
        for reach in range(1, 5):
            ahead = shifted(extended, along, reach, sizes)
            behind = shifted(extended, along, -reach, sizes)
            laplace = laplace + second_coef[reach] * (ahead + behind)
            slope = slope + first_coef[reach - 1] * (ahead - behind)
        firsts.append(slope)
    return laplace, firsts


def operator_apply(padded, buoyancy, slopes):
    laplace, firsts = derivatives(padded)
    return buoyancy * laplace + slopes[0] * firsts[0] + slopes[1] * firsts[1] + slopes[2] * firsts[2]


def pad_sides(field):
    return jnp.pad(field, ((4, 4), (4, 4), (0, 0)))


def reference(stiffness, buoyancy, fwd_prev, fwd_now, adj_prev, adj_now, wavelet, source_cell, receiver_cell, traces, aperture_blocks, aperture_count):
    unused, slopes = derivatives(pad_sides(buoyancy))

    def one_shot(items):
        prev, now, aprev, anow, wave, source, cells, trace = items
        forward = [prev, now]
        adjoint = [aprev, anow]
        for step_index in range(STEPS):
            source_field = jnp.zeros((NX, NY, NZ), jnp.float32).at[source[0], source[1], source[2]].add(wave[step_index])
            record_field = jnp.zeros((NX, NY, NZ), jnp.float32).at[cells[:, 0], cells[:, 1], cells[:, 2]].add(trace[:, step_index])
            forward.append(2.0 * forward[-1] - forward[-2] + stiffness * operator_apply(pad_sides(forward[-1]), buoyancy, slopes) + source_field)
            adjoint.append(2.0 * adjoint[-1] - adjoint[-2] + stiffness * operator_apply(pad_sides(adjoint[-1]), buoyancy, slopes) + record_field)
        image = jnp.zeros((NX, NY, NZ), jnp.float32)
        for later in range(2, STEPS + 2):
            image = image + adjoint[later] * (forward[STEPS + 3 - later] - 2.0 * forward[STEPS + 2 - later] + forward[STEPS + 1 - later])
        coarse = image.reshape(NXC, 2, NYC, 2, NZC, 2).mean(axis=(1, 3, 5))
        return forward[-1], adjoint[-1], coarse

    fwd_final, adj_final, coarse_all = lax.map(one_shot, (fwd_prev, fwd_now, adj_prev, adj_now, wavelet, source_cell, receiver_cell, traces))
    rows_own = NXC // N_GX // N_SHOT
    valid = jnp.arange(aperture_blocks.shape[4])[None, None, None, None, :] < aperture_count[..., None]
    hits = jnp.any((aperture_blocks[..., None] == jnp.arange(rows_own)[None, None, None, None, None, :]) & valid[..., None], axis=4)
    mask = hits.reshape(SHOTS, N_GX, N_GY, NXC // N_GX).astype(jnp.float32)
    mask = jnp.transpose(mask, (0, 1, 3, 2))
    shaped = coarse_all.reshape(SHOTS, N_GX, NXC // N_GX, N_GY, NYC // N_GY, NZC)
    gradient = jnp.sum(shaped * mask[:, :, :, :, None, None], axis=0)
    return fwd_final, adj_final, gradient.reshape(N_GX, NXC // N_GX, NYC, NZC)
```

```python
import jax
import jax.numpy as jnp
from jax import lax
from jax.experimental import pallas as pl
from jax.experimental.pallas import tpu as pltpu
from jax.sharding import PartitionSpec as P

MESH = pl.DeviceIdType.MESH
STEPS = 4
WIDTH = 4
CHUNK = 6
TOP = 8
LANES = 128

C1, D1 = 8.0 / 5.0, 4.0 / 5.0
second = tuple(c / C1 for c in (-205.0 / 72.0, 8.0 / 5.0, -1.0 / 5.0, 8.0 / 315.0, -1.0 / 560.0))
first = tuple(d / D1 for d in (4.0 / 5.0, -1.0 / 5.0, 4.0 / 105.0, -1.0 / 280.0))


def split(v):
    high = v.astype(jnp.bfloat16)
    return high, (v - high.astype(jnp.float32)).astype(jnp.bfloat16)


def dot(a, b):
    return jnp.dot(a, b, preferred_element_type=jnp.float32)


def dot_nt(a, b):
    return lax.dot_general(a, b, (((1,), (1,)), ((), ())), preferred_element_type=jnp.float32)


def kernel(
    stiff, buoy, fwd0, fwd1, adj0, adj1, wave, source, receiver, traces, blocks, counts,
    fwd_out, adj_out, grad_out,
    F, B, K, CO, R, Q, A, BH, BL, CZ, PZ, ZS, SM, TI, OUTG, INC,
    load_sem, bx_send, bx_recv, by_send, by_recv, x_send, x_recv, y_send, y_recv,
    out_sem, g_send, g_recv,
):
    nx, ny, nz = stiff.shape
    chunks = nx // CHUNK
    gx, gy, me = lax.axis_index("gx"), lax.axis_index("gy"), lax.axis_index("shot")
    last_x, last_y = lax.axis_size("gx") - 1, lax.axis_size("gy") - 1
    shots = lax.axis_size("shot")
    own = pl.ds(TOP, ny)
    sides_x = ((gx > 0, gx - 1), (gx < last_x, gx + 1))
    sides_y = ((gy > 0, gy - 1), (gy < last_y, gy + 1))

    loads = []
    for half in range(2):
        z = pl.ds(half * LANES, LANES)
        inner = pl.ds(WIDTH, nx)
        loads += [
            (buoy.at[:, :, z], B.at[inner, half, own, :]),
            (fwd1.at[0, :, :, z], F.at[1, 0, inner, half, own, :]),
            (adj1.at[0, :, :, z], F.at[1, 1, inner, half, own, :]),
            (stiff.at[:, :, z], K.at[:, half]),
            (fwd0.at[0, :, :, z], F.at[0, 0, inner, half, own, :]),
            (adj0.at[0, :, :, z], F.at[0, 1, inner, half, own, :]),
        ]
    loads = [pltpu.make_async_copy(s, d, load_sem.at[i]) for i, (s, d) in enumerate(loads)]
    for i in (0, 6, 1, 7, 2, 8, 3, 9, 4, 10, 5, 11):
        loads[i].start()

    barrier = pltpu.get_barrier_semaphore()
    peers = shots - 1
    for axis, sides in (("gx", sides_x), ("gy", sides_y)):
        for there, index in sides:
            @pl.when(there)
            def _():
                pl.semaphore_signal(barrier, inc=1, device_id={axis: index}, device_id_type=MESH)
            peers = peers + jnp.where(there, 1, 0)

    def greet(step, _):
        pl.semaphore_signal(
            barrier, inc=1, device_id={"shot": lax.rem(me + step, shots)}, device_id_type=MESH
        )
        return 0

    lax.fori_loop(1, shots, greet, 0)

    for side, (there, _) in enumerate(sides_x):
        @pl.when(jnp.logical_not(there))
        def _():
            at = pl.ds(side * (nx + WIDTH), WIDTH)
            B[at, :, own, :] = jnp.zeros((WIDTH, 2, ny, LANES), jnp.float32)
            for level in range(1, STEPS + 1):
                for field in range(2):
                    F[level, field, at, :, own, :] = jnp.zeros((WIDTH, 2, ny, LANES), jnp.float32)
    for side, (there, _) in enumerate(sides_y):
        @pl.when(jnp.logical_not(there))
        def _():
            at = pl.ds(TOP - WIDTH + side * (ny + WIDTH), WIDTH)

            def clear(x, _):
                B[x, :, at, :] = jnp.zeros((2, WIDTH, LANES), jnp.float32)
                for level in range(1, STEPS + 1):
                    for field in range(2):
                        F[level, field, x, :, at, :] = jnp.zeros((2, WIDTH, LANES), jnp.float32)
                return 0

            lax.fori_loop(WIDTH, nx + WIDTH, clear, 0)

    def x_edge(side):
        return pl.ds(WIDTH + side * (nx - WIDTH), WIDTH), pl.ds((1 - side) * (nx + WIDTH), WIDTH)

    def y_edge(side):
        return (
            pl.ds(TOP + side * (ny - WIDTH), WIDTH),
            pl.ds(TOP - WIDTH + (1 - side) * (ny + WIDTH), WIDTH),
        )

    def x_copy(level, side, index):
        mine, theirs = x_edge(side)
        return pltpu.make_async_remote_copy(
            src_ref=F.at[level, :, mine, :, own, :],
            dst_ref=F.at[level, :, theirs, :, own, :],
            send_sem=x_send.at[level, side],
            recv_sem=x_recv.at[level, 1 - side],
            device_id={"gx": index},
            device_id_type=MESH,
        )

    def x_arrival(level, side, index):
        _, here = x_edge(1 - side)
        return pltpu.make_async_remote_copy(
            src_ref=F.at[level, :, here, :, own, :],
            dst_ref=F.at[level, :, here, :, own, :],
            send_sem=x_send.at[level, side],
            recv_sem=x_recv.at[level, side],
            device_id={"gx": index},
            device_id_type=MESH,
        )

    def y_copy(level, chunk, side, index):
        mine, theirs = y_edge(side)
        x = pl.ds(WIDTH + chunk * CHUNK, CHUNK)
        return pltpu.make_async_remote_copy(
            src_ref=F.at[level, :, x, :, mine, :],
            dst_ref=F.at[level, :, x, :, theirs, :],
            send_sem=y_send.at[level, chunk, side],
            recv_sem=y_recv.at[level, chunk, 1 - side],
            device_id={"gy": index},
            device_id_type=MESH,
        )

    def y_arrival(level, chunk, side, index):
        _, here = y_edge(1 - side)
        x = pl.ds(WIDTH + chunk * CHUNK, CHUNK)
        return pltpu.make_async_remote_copy(
            src_ref=F.at[level, :, x, :, here, :],
            dst_ref=F.at[level, :, x, :, here, :],
            send_sem=y_send.at[level, chunk, side],
            recv_sem=y_recv.at[level, chunk, side],
            device_id={"gy": index},
            device_id_type=MESH,
        )

    def bx_copy(side, index, arrival=False):
        mine, theirs = x_edge(1 - side if arrival else side)
        return pltpu.make_async_remote_copy(
            src_ref=B.at[theirs if arrival else mine, :, own, :],
            dst_ref=B.at[theirs, :, own, :],
            send_sem=bx_send.at[side],
            recv_sem=bx_recv.at[side if arrival else 1 - side],
            device_id={"gx": index},
            device_id_type=MESH,
        )

    def by_copy(chunk, side, index, arrival=False):
        mine, theirs = y_edge(1 - side if arrival else side)
        x = pl.ds(WIDTH + chunk * CHUNK, CHUNK)
        return pltpu.make_async_remote_copy(
            src_ref=B.at[x, :, theirs if arrival else mine, :],
            dst_ref=B.at[x, :, theirs, :],
            send_sem=by_send.at[chunk, side],
            recv_sem=by_recv.at[chunk, side if arrival else 1 - side],
            device_id={"gy": index},
            device_id_type=MESH,
        )

    def for_sides(sides, do):
        for side, (there, index) in enumerate(sides):
            @pl.when(there)
            def _():
                do(side, index)

    def order(i):
        return lax.rem(chunks - i, chunks)

    for i in (0, 6, 1, 7, 2, 8):
        loads[i].wait()
    pl.semaphore_wait(barrier, peers)
    for_sides(sides_x, lambda side, index: bx_copy(side, index).start())
    for_sides(sides_x, lambda side, index: x_copy(1, side, index).start())

    def first_strips(i, _):
        chunk = order(i)

        def go(side, index):
            by_copy(chunk, side, index).start()
            y_copy(1, chunk, side, index).start()

        for_sides(sides_y, go)
        return 0

    lax.fori_loop(0, chunks, first_strips, 0)

    diff = lax.broadcasted_iota(jnp.int32, (nz, nz), 0) - lax.broadcasted_iota(jnp.int32, (nz, nz), 1)
    lap = jnp.zeros((nz, nz), jnp.float32)
    der = jnp.zeros((nz, nz), jnp.float32)
    for reach in range(1, WIDTH + 1):
        lap = jnp.where(jnp.abs(diff) == reach, second[reach], lap)
        der = jnp.where(diff == reach, first[reach - 1], der)
        der = jnp.where(diff == -reach, -first[reach - 1], der)
    CZ[:, 0:nz] = lap.astype(jnp.bfloat16)
    CZ[:, nz:] = der.astype(jnp.bfloat16)
    fine = lax.broadcasted_iota(jnp.int32, (nz, nz // 2), 0)
    pair = lax.broadcasted_iota(jnp.int32, (nz, nz // 2), 1) * 2
    PZ[...] = jnp.where((fine == pair) | (fine == pair + 1), 0.125, 0.0).astype(jnp.bfloat16)

    for half in range(2):
        row = lax.broadcasted_iota(jnp.int32, (ny, LANES), 0) + gy * ny
        col = lax.broadcasted_iota(jnp.int32, (ny, LANES), 1) + half * LANES
        SM[half] = jnp.where((row == source[0, 1]) & (col == source[0, 2]), 1.0, 0.0)

    rec_x = receiver[0] - gx * nx
    rec_y = receiver[1] - gy * ny
    inside = (rec_x >= 0) & (rec_x < nx) & (rec_y >= 0) & (rec_y < ny)
    cell = jnp.where(inside, rec_x * ny + rec_y, -1)
    nrec = cell.shape[1]
    rows = 128

    def hot(g, _):
        at = lax.broadcasted_iota(jnp.int32, (rows, nrec), 0) + g * rows
        A[pl.ds(pl.multiple_of(g * rows, rows), rows), :] = jnp.where(at == cell, 1.0, 0.0).astype(
            jnp.bfloat16
        )
        return 0

    lax.fori_loop(0, nx * ny // rows, hot, 0)
    rec_z = receiver[2]
    for n in range(STEPS):
        def place(g, _):
            at = lax.broadcasted_iota(jnp.int32, (64, nrec), 0) + g * 64
            high, low = split(jnp.where(at == rec_z, traces[0, n : n + 1, :], 0.0))
            where = pl.ds(pl.multiple_of(g * 64, 64), 64)
            BH[n, where, :] = high
            BL[n, where, :] = low
            return 0

        lax.fori_loop(0, nz // 64, place, 0)

    def inject(n, _):
        for part in range(2):
            hots = A[pl.ds(part * nx * ny // 2, nx * ny // 2), :]
            field = dot_nt(hots, BH[n]) + dot_nt(hots, BL[n])
            field = field.reshape(nx // 2, ny, nz)
            for half in range(2):
                R[n, pl.ds(part * nx // 2, nx // 2), half] = field[:, :, half * LANES : (half + 1) * LANES]
        return 0

    lax.fori_loop(0, STEPS, inject, 0)

    for i in (3, 9, 4, 10, 5, 11):
        loads[i].wait()

    def both_halves(ref, x):
        parts = [ref[x, half, own, :].reshape(CHUNK * ny, LANES) for half in range(2)]
        return jnp.concatenate(parts, axis=1)

    def slopes(ref, along, x, half):
        total = None
        for reach in range(1, WIDTH + 1):
            if along == 0:
                ahead, behind = ref[x + reach, half, own, :], ref[x - reach, half, own, :]
            else:
                ahead = ref[x, half, pl.ds(TOP + reach, ny), :]
                behind = ref[x, half, pl.ds(TOP - reach, ny), :]
            term = ahead - behind
            if reach > 1:
                term = first[reach - 1] * term
            total = term if total is None else total + term
        return total

    def coefficients(chunk):
        @pl.when(chunk == 0)
        def _():
            @pl.when(sides_x[0][0])
            def _():
                bx_copy(0, sides_x[0][1], True).wait_recv()

        @pl.when(chunk == chunks - 1)
        def _():
            @pl.when(sides_x[1][0])
            def _():
                bx_copy(1, sides_x[1][1], True).wait_recv()

        for_sides(sides_y, lambda side, index: by_copy(chunk, side, index, True).wait_recv())
        x0 = chunk * CHUNK
        high, low = split(both_halves(B, pl.ds(WIDTH + x0, CHUNK)))
        der_z = dot(high, CZ[:, nz:]) + dot(low, CZ[:, nz:])
        for half in range(2):
            ZS[0, 0, half] = der_z[:, half * LANES : (half + 1) * LANES]

        def plane(j, _):
            x = x0 + j
            for half in range(2):
                stiffness = K[x, half]
                CO[0, x, half] = C1 * stiffness * B[WIDTH + x, half, own, :]
                stiffness = (D1 * D1) * stiffness
                CO[1, x, half] = stiffness * slopes(B, 0, WIDTH + x, half)
                CO[2, x, half] = stiffness * slopes(B, 1, WIDTH + x, half)
                at = pl.ds(pl.multiple_of(j * ny, ny), ny)
                CO[3, x, half] = stiffness * ZS[0, 0, half, at, :]
            return 0

        lax.fori_loop(0, CHUNK, plane, 0)

    def advance(n, chunk):
        level = n + 1
        x0 = chunk * CHUNK

        @pl.when(chunk == 0)
        def _():
            @pl.when(sides_x[0][0])
            def _():
                x_arrival(level, 0, sides_x[0][1]).wait_recv()

        @pl.when(chunk == chunks - 1)
        def _():
            @pl.when(sides_x[1][0])
            def _():
                x_arrival(level, 1, sides_x[1][1]).wait_recv()

        for_sides(sides_y, lambda side, index: y_arrival(level, chunk, side, index).wait_recv())

        inner = pl.ds(WIDTH + x0, CHUNK)
        both = [both_halves(F.at[level, field], inner) for field in range(2)]
        high, low = split(jnp.concatenate(both, axis=0))
        along_z = dot(high, CZ[...]) + dot(low, CZ[...])
        for field in range(2):
            for kind in range(2):
                for half in range(2):
                    c0 = kind * nz + half * LANES
                    r0 = field * CHUNK * ny
                    ZS[field, kind, half] = along_z[r0 : r0 + CHUNK * ny, c0 : c0 + LANES]

        def plane(j, _):
            x = x0 + j
            xe = x + WIDTH
            at = pl.ds(pl.multiple_of(j * ny, ny), ny)
            amplitude = jnp.where(source[0, 0] - gx * nx == x, wave[0, n], 0.0)
            for half in range(2):
                co = [CO[i, x, half] for i in range(4)]
                for field in range(2):
                    ref = F.at[level, field]
                    now = ref[xe, half, own, :]
                    lap = (3.0 * second[0]) * now + ZS[field, 0, half, at, :]
                    der_x = der_y = None
                    for reach in range(1, WIDTH + 1):
                        xa, xb = ref[xe + reach, half, own, :], ref[xe - reach, half, own, :]
                        ya = ref[xe, half, pl.ds(TOP + reach, ny), :]
                        yb = ref[xe, half, pl.ds(TOP - reach, ny), :]
                        pairs = (xa + xb) + (ya + yb)
                        dx, dy = xa - xb, ya - yb
                        if reach == 1:
                            lap, der_x, der_y = lap + pairs, dx, dy
                        else:
                            lap = lap + second[reach] * pairs
                            der_x = der_x + first[reach - 1] * dx
                            der_y = der_y + first[reach - 1] * dy
                    change = co[0] * lap + co[1] * der_x + co[2] * der_y
                    change = change + co[3] * ZS[field, 1, half, at, :]
                    if field == 0:
                        change = change + amplitude * SM[half]
                        Q[n, x, half] = change
                    else:
                        change = change + R[n, x, half]
                    before = F[n, field, xe, half, own, :]
                    F[n + 2, field, xe, half, own, :] = (2.0 * now - before) + change
            return 0

        lax.fori_loop(0, CHUNK, plane, 0)

        @pl.when(n < STEPS - 1)
        def _():
            @pl.when(chunk == 0)
            def _():
                @pl.when(sides_x[0][0])
                def _():
                    x_copy(level + 1, 0, sides_x[0][1]).start()

            @pl.when(chunk == chunks - 1)
            def _():
                @pl.when(sides_x[1][0])
                def _():
                    x_copy(level + 1, 1, sides_x[1][1]).start()

            for_sides(sides_y, lambda side, index: y_copy(level + 1, chunk, side, index).start())

    def out_copies(chunk):
        x = pl.ds(chunk * CHUNK, CHUNK)
        xe = pl.ds(WIDTH + chunk * CHUNK, CHUNK)
        for field, out in enumerate((fwd_out, adj_out)):
            for half in range(2):
                yield pltpu.make_async_copy(
                    F.at[STEPS + 1, field, xe, half, own, :],
                    out.at[0, x, :, pl.ds(half * LANES, LANES)],
                    out_sem.at[chunk, field, half],
                )

    def grad_copy(owner, slot, sem):
        return pltpu.make_async_remote_copy(
            src_ref=OUTG.at[owner],
            dst_ref=INC.at[slot],
            send_sem=g_send.at[owner],
            recv_sem=g_recv.at[sem],
            device_id={"shot": owner},
            device_id_type=MESH,
        )

    def chosen(shot, owner, k):
        valid = (blocks[shot, gx, gy, 0, owner] == k) & (counts[shot, gx, gy, owner] > 0)
        return jnp.where(valid, 1.0, 0.0)

    def imaging(chunk):
        for copy in out_copies(chunk):
            copy.start()
        x0 = chunk * CHUNK
        for k in range(CHUNK // 2):
            for half in range(2):
                total = None
                for odd in range(2):
                    x = x0 + 2 * k + odd
                    for later in range(2, STEPS + 2):
                        term = F[later, 1, x + WIDTH, half, own, :] * Q[STEPS + 1 - later, x, half]
                        total = term if total is None else total + term
                TI[k, half] = total
        rows_k = []
        for k in range(CHUNK // 2):
            halves = [
                TI[k, half, pl.ds(0, ny // 2, stride=2), :] + TI[k, half, pl.ds(1, ny // 2, stride=2), :]
                for half in range(2)
            ]
            rows_k.append(jnp.concatenate(halves, axis=1))
        high, low = split(jnp.concatenate(rows_k, axis=0))
        coarse = dot(high, PZ[...]) + dot(low, PZ[...])
        row = None
        for k in range(CHUNK // 2):
            term = chosen(me, chunk, k) * coarse[k * (ny // 2) : (k + 1) * (ny // 2), :]
            row = term if row is None else row + term

        @pl.when(chunk == me)
        def _():
            INC[me] = row

        @pl.when(chunk != me)
        def _():
            OUTG[chunk] = row
            grad_copy(chunk, me, me).start()

    def run(t, _):
        n = t // chunks
        chunk = order(lax.rem(t, chunks))

        @pl.when(n == 0)
        def _():
            coefficients(chunk)

        advance(n, chunk)

        @pl.when(n == STEPS - 1)
        def _():
            imaging(chunk)

        return 0

    lax.fori_loop(0, STEPS * chunks, run, 0)

    def arrive(step, _):
        shot = lax.rem(me + step, shots)
        grad_copy(shot, shot, shot).wait_recv()
        return 0

    lax.fori_loop(1, shots, arrive, 0)
    for k in range(CHUNK // 2):
        total = None
        for shot in range(shots):
            term = chosen(shot, me, k) * INC[shot]
            total = term if total is None else total + term
        grad_out[0, k] = total

    def sent(step, _):
        grad_copy(lax.rem(me + step, shots), me, me).wait_send()
        return 0

    lax.fori_loop(1, shots, sent, 0)

    def done(chunk, _):
        for copy in out_copies(chunk):
            copy.wait()

        def strips(side, index):
            by_copy(chunk, side, index).wait_send()
            for level in range(1, STEPS + 1):
                y_copy(level, chunk, side, index).wait_send()

        for_sides(sides_y, strips)
        return 0

    lax.fori_loop(0, chunks, done, 0)

    def faces(side, index):
        bx_copy(side, index).wait_send()
        for level in range(1, STEPS + 1):
            x_copy(level, side, index).wait_send()

    for_sides(sides_x, faces)


def body(
    stiffness, buoyancy, fwd_prev, fwd_now, adj_prev, adj_now, wavelet, source_cell, receiver_cell,
    traces, aperture_blocks, aperture_count,
):
    nx, ny, nz = stiffness.shape
    shots = lax.axis_size("shot")
    nrec = traces.shape[1]
    chunks = nx // CHUNK
    xe, ye = nx + 2 * WIDTH, ny + 2 * TOP
    f32, bf16 = jnp.float32, jnp.bfloat16
    hbm = pl.BlockSpec(memory_space=pl.ANY)
    vmem = pl.BlockSpec(memory_space=pltpu.VMEM)
    smem = pl.BlockSpec(memory_space=pltpu.SMEM)
    dma = pltpu.SemaphoreType.DMA
    return pl.pallas_call(
        kernel,
        out_shape=(
            jax.ShapeDtypeStruct(fwd_now.shape, f32),
            jax.ShapeDtypeStruct(adj_now.shape, f32),
            jax.ShapeDtypeStruct((1, nx // 2 // shots, ny // 2, nz // 2), f32),
        ),
        in_specs=[hbm] * 6 + [smem] * 2 + [vmem] * 2 + [smem] * 2,
        out_specs=(hbm, hbm, vmem),
        scratch_shapes=[
            pltpu.VMEM((STEPS + 2, 2, xe, 2, ye, LANES), f32),
            pltpu.VMEM((xe, 2, ye, LANES), f32),
            pltpu.VMEM((nx, 2, ny, LANES), f32),
            pltpu.VMEM((4, nx, 2, ny, LANES), f32),
            pltpu.VMEM((STEPS, nx, 2, ny, LANES), f32),
            pltpu.VMEM((STEPS, nx, 2, ny, LANES), f32),
            pltpu.VMEM((nx * ny, nrec), bf16),
            pltpu.VMEM((STEPS, nz, nrec), bf16),
            pltpu.VMEM((STEPS, nz, nrec), bf16),
            pltpu.VMEM((nz, 2 * nz), bf16),
            pltpu.VMEM((nz, nz // 2), bf16),
            pltpu.VMEM((2, 2, 2, CHUNK * ny, LANES), f32),
            pltpu.VMEM((2, ny, LANES), f32),
            pltpu.VMEM((CHUNK // 2, 2, ny, LANES), f32),
            pltpu.VMEM((shots, ny // 2, nz // 2), f32),
            pltpu.VMEM((shots, ny // 2, nz // 2), f32),
            dma((12,)),
            dma((2,)),
            dma((2,)),
            dma((chunks, 2)),
            dma((chunks, 2)),
            dma((STEPS + 1, 2)),
            dma((STEPS + 1, 2)),
            dma((STEPS + 1, chunks, 2)),
            dma((STEPS + 1, chunks, 2)),
            dma((chunks, 2, 2)),
            dma((shots,)),
            dma((shots,)),
        ],
        compiler_params=pltpu.CompilerParams(
            collective_id=0, has_side_effects=True, vmem_limit_bytes=52 << 20
        ),
        name="window",
    )(
        stiffness, buoyancy, fwd_prev, fwd_now, adj_prev, adj_now, wavelet, source_cell,
        jnp.transpose(receiver_cell, (2, 0, 1)),
        jnp.transpose(traces, (0, 2, 1)),
        jnp.swapaxes(aperture_blocks, 3, 4),
        aperture_count,
    )


def solution(mesh):
    in_specs = (
        P("gx", "gy", None),
        P("gx", "gy", None),
        P("shot", "gx", "gy", None),
        P("shot", "gx", "gy", None),
        P("shot", "gx", "gy", None),
        P("shot", "gx", "gy", None),
        P("shot", None),
        P("shot", None),
        P("shot", None, None),
        P("shot", None, None),
        P(),
        P(),
    )
    out_specs = (
        P("shot", "gx", "gy", None),
        P("shot", "gx", "gy", None),
        P("gx", "shot", "gy", None),
    )
    return jax.shard_map(body, mesh=mesh, in_specs=in_specs, out_specs=out_specs, check_vma=False)
```

```python
import jax
import jax.numpy as jnp
from jax import lax
from jax.experimental import pallas as pl
from jax.experimental.pallas import tpu as pltpu
from jax.sharding import PartitionSpec as P

MESH = pl.DeviceIdType.MESH
STEPS = 4
WIDTH = 4
BLOCK = 24
CHUNK = 6
TOP = 8
LANES = 128

C1, D1 = 8.0 / 5.0, 4.0 / 5.0
second = tuple(c / C1 for c in (-205.0 / 72.0, 8.0 / 5.0, -1.0 / 5.0, 8.0 / 315.0, -1.0 / 560.0))
first = tuple(d / D1 for d in (4.0 / 5.0, -1.0 / 5.0, 4.0 / 105.0, -1.0 / 280.0))


def split(v):
    high = v.astype(jnp.bfloat16)
    return high, (v - high.astype(jnp.float32)).astype(jnp.bfloat16)


def dot(a, b):
    return jnp.dot(a, b, preferred_element_type=jnp.float32)


def dot_nt(a, b):
    return lax.dot_general(a, b, (((1,), (1,)), ((), ())), preferred_element_type=jnp.float32)


def kernel(
    stiff, buoy, fwd0, fwd1, adj0, adj1, wave_in, source_in, receiver_in, traces_in, blocks_in, counts_in,
    fwd_out, adj_out, grad_out,
    F0, F1, F2, F3, F4, F5, K, CO, R, Q, A, BH, BL, CZ, PZ, Z0, Z1, SM, TI, OUTG, INC,
    receiver, traces, wave, source, blocks, counts,
    load_sem, x_send, x_recv, y_send, y_recv, out_sem, g_send, g_recv,
):
    levels = (F0, F1, F2, F3, F4, F5)
    depth = (Z0, Z1)
    B = F1.at[2]
    nx, ny, nz = stiff.shape
    chunks = nx // CHUNK
    gx, gy, me = lax.axis_index("gx"), lax.axis_index("gy"), lax.axis_index("shot")
    last_x, last_y = lax.axis_size("gx") - 1, lax.axis_size("gy") - 1
    shots = lax.axis_size("shot")
    own = pl.ds(TOP, ny)
    inner = pl.ds(WIDTH, nx)
    sides_x = ((gx > 0, gx - 1), (gx < last_x, gx + 1))
    sides_y = ((gy > 0, gy - 1), (gy < last_y, gy + 1))

    def for_sides(sides, do):
        for side, (there, index) in enumerate(sides):
            @pl.when(there)
            def _():
                do(side, index)

    barrier = pltpu.get_barrier_semaphore()
    peers = shots - 1
    for axis, sides in (("gx", sides_x), ("gy", sides_y)):
        for there, index in sides:
            @pl.when(there)
            def _():
                pl.semaphore_signal(barrier, inc=1, device_id={axis: index}, device_id_type=MESH)
            peers = peers + jnp.where(there, 1, 0)

    def greet(step, _):
        pl.semaphore_signal(
            barrier, inc=1, device_id={"shot": lax.rem(me + step, shots)}, device_id_type=MESH
        )
        return 0

    lax.fori_loop(1, shots, greet, 0)

    small = [
        pltpu.make_async_copy(src, dst, load_sem.at[6 + i])
        for i, (src, dst) in enumerate(
            (
                (receiver_in, receiver),
                (traces_in, traces),
                (wave_in, wave),
                (source_in, source),
                (blocks_in.at[:, gx, gy], blocks),
                (counts_in.at[:, gx], counts),
            )
        )
    ]
    large = (
        (buoy, F1.at[2, inner, :, own, :]),
        (fwd1.at[0], F1.at[0, inner, :, own, :]),
        (adj1.at[0], F1.at[1, inner, :, own, :]),
        (stiff, K),
        (fwd0.at[0], F0.at[0, inner, :, own, :]),
        (adj0.at[0], F0.at[1, inner, :, own, :]),
    )

    def load(i):
        src, dst = large[i]
        for half in range(2):
            pltpu.make_async_copy(
                src.at[:, :, pl.ds(half * LANES, LANES)], dst.at[:, half], load_sem.at[i]
            ).start()

    def loaded(i):
        dst = large[i][1]
        pltpu.make_async_copy(dst, dst, load_sem.at[i]).wait()

    for copy in small[:4]:
        copy.start()
    for i in range(6):
        load(i)
    for copy in small[4:]:
        copy.start()

    for side, (there, _) in enumerate(sides_x):
        @pl.when(jnp.logical_not(there))
        def _():
            at = pl.ds(side * (nx + WIDTH), WIDTH)
            for ref in levels[1 : STEPS + 1]:
                for field in range(ref.shape[0]):
                    ref[field, at, :, own, :] = jnp.zeros((WIDTH, 2, ny, LANES), jnp.float32)
    for side, (there, _) in enumerate(sides_y):
        @pl.when(jnp.logical_not(there))
        def _():
            at = pl.ds(TOP - WIDTH + side * (ny + WIDTH), WIDTH)

            def clear(x, _):
                for ref in levels[1 : STEPS + 1]:
                    for field in range(ref.shape[0]):
                        ref[field, x, :, at, :] = jnp.zeros((2, WIDTH, LANES), jnp.float32)
                return 0

            lax.fori_loop(WIDTH, nx + WIDTH, clear, 0)

    def x_edge(side):
        return pl.ds(WIDTH + side * (nx - WIDTH), WIDTH), pl.ds((1 - side) * (nx + WIDTH), WIDTH)

    def y_edge(side):
        return (
            pl.ds(TOP + side * (ny - WIDTH), WIDTH),
            pl.ds(TOP - WIDTH + (1 - side) * (ny + WIDTH), WIDTH),
        )

    def x_copy(level, side, index, arrival=False):
        ref = levels[level]
        mine, theirs = x_edge(1 - side if arrival else side)
        return pltpu.make_async_remote_copy(
            src_ref=ref.at[:, theirs if arrival else mine, :, own, :],
            dst_ref=ref.at[:, theirs, :, own, :],
            send_sem=x_send.at[side],
            recv_sem=x_recv.at[level % 2, side if arrival else 1 - side],
            device_id={"gx": index},
            device_id_type=MESH,
        )

    def y_copy(level, chunk, side, index, arrival=False):
        ref = levels[level]
        mine, theirs = y_edge(1 - side if arrival else side)
        x = pl.ds(WIDTH + chunk * CHUNK, CHUNK)
        return pltpu.make_async_remote_copy(
            src_ref=ref.at[:, x, :, theirs if arrival else mine, :],
            dst_ref=ref.at[:, x, :, theirs, :],
            send_sem=y_send.at[chunk, side],
            recv_sem=y_recv.at[level % 2, chunk, side if arrival else 1 - side],
            device_id={"gy": index},
            device_id_type=MESH,
        )

    def order(i):
        return lax.rem(chunks - i, chunks)

    def on_border(chunk, do):
        for side, border in enumerate((0, chunks - 1)):
            there, index = sides_x[side]

            @pl.when((chunk == border) & there)
            def _():
                do(side, index)

    def await_halos(level, chunk):
        on_border(chunk, lambda side, index: x_copy(level, side, index, True).wait_recv())
        for_sides(sides_y, lambda side, index: y_copy(level, chunk, side, index, True).wait_recv())

    diff = lax.broadcasted_iota(jnp.int32, (nz, nz), 0) - lax.broadcasted_iota(jnp.int32, (nz, nz), 1)
    lap = jnp.zeros((nz, nz), jnp.float32)
    der = jnp.zeros((nz, nz), jnp.float32)
    for reach in range(1, WIDTH + 1):
        lap = jnp.where(jnp.abs(diff) == reach, second[reach], lap)
        der = jnp.where(diff == reach, first[reach - 1], der)
        der = jnp.where(diff == -reach, -first[reach - 1], der)
    CZ[:, 0:nz] = lap.astype(jnp.bfloat16)
    CZ[:, nz:] = der.astype(jnp.bfloat16)
    fine = lax.broadcasted_iota(jnp.int32, (nz, nz // 2), 0)
    pair = lax.broadcasted_iota(jnp.int32, (nz, nz // 2), 1) * 2
    PZ[...] = jnp.where((fine == pair) | (fine == pair + 1), 0.125, 0.0).astype(jnp.bfloat16)

    for copy in small[:4]:
        copy.wait()

    for half in range(2):
        row = lax.broadcasted_iota(jnp.int32, (ny, LANES), 0) + gy * ny
        col = lax.broadcasted_iota(jnp.int32, (ny, LANES), 1) + half * LANES
        SM[half] = jnp.where((row == source[0, 1]) & (col == source[0, 2]), 1.0, 0.0)

    rec_x = receiver[0] - gx * nx
    rec_y = receiver[1] - gy * ny
    inside = (rec_x >= 0) & (rec_x < nx) & (rec_y >= 0) & (rec_y < ny)
    cell = jnp.where(inside, rec_x * ny + rec_y, -1)
    nrec = cell.shape[1]
    rows = 128

    def hot(g, _):
        at = lax.broadcasted_iota(jnp.int32, (rows, nrec), 0) + g * rows
        A[pl.ds(pl.multiple_of(g * rows, rows), rows), :] = jnp.where(at == cell, 1.0, 0.0).astype(
            jnp.bfloat16
        )
        return 0

    lax.fori_loop(0, nx * ny // rows, hot, 0)
    rec_z = receiver[2]
    for n in range(STEPS):
        def place(g, _):
            at = lax.broadcasted_iota(jnp.int32, (64, nrec), 0) + g * 64
            high, low = split(jnp.where(at == rec_z, traces[0, n : n + 1, :], 0.0))
            where = pl.ds(pl.multiple_of(g * 64, 64), 64)
            BH[n, where, :] = high
            BL[n, where, :] = low
            return 0

        lax.fori_loop(0, nz // 64, place, 0)

    def inject(n, _):
        for part in range(2):
            hots = A[pl.ds(part * nx * ny // 2, nx * ny // 2), :]
            field = dot_nt(hots, BH[n]) + dot_nt(hots, BL[n])
            field = field.reshape(nx // 2, ny, nz)
            for half in range(2):
                R[n, pl.ds(part * nx // 2, nx // 2), half] = field[:, :, half * LANES : (half + 1) * LANES]
        return 0

    lax.fori_loop(0, STEPS, inject, 0)

    for i in range(3):
        loaded(i)
    pl.semaphore_wait(barrier, peers)
    for_sides(sides_x, lambda side, index: x_copy(1, side, index).start())

    def first_strips(i, _):
        for_sides(sides_y, lambda side, index: y_copy(1, order(i), side, index).start())
        return 0

    lax.fori_loop(0, chunks, first_strips, 0)

    def along_depth(ref, block, out_ref):
        x = pl.ds(WIDTH + block * BLOCK, BLOCK)
        cells = BLOCK * ny
        parts = [
            jnp.concatenate(
                [ref[field, x, half, own, :].reshape(cells, LANES) for half in range(2)], axis=1
            )
            for field in range(2)
        ]
        high, low = split(jnp.concatenate(parts, axis=0))
        out = dot(high, CZ[...]) + dot(low, CZ[...])
        for field in range(2):
            for kind in range(2):
                for half in range(2):
                    at = kind * nz + half * LANES
                    piece = out[field * cells : (field + 1) * cells, at : at + LANES]
                    out_ref[field, kind, pl.ds(block * BLOCK, BLOCK), half] = piece.reshape(
                        BLOCK, ny, LANES
                    )

    def slopes(along, x, half):
        total = None
        for reach in range(1, WIDTH + 1):
            if along == 0:
                ahead, behind = B[x + reach, half, own, :], B[x - reach, half, own, :]
            else:
                ahead = B[x, half, pl.ds(TOP + reach, ny), :]
                behind = B[x, half, pl.ds(TOP - reach, ny), :]
            term = ahead - behind
            if reach > 1:
                term = first[reach - 1] * term
            total = term if total is None else total + term
        return total

    loaded(3)

    def prepare(chunk, _):
        x = pl.ds(WIDTH + chunk * CHUNK, CHUNK)
        xk = pl.ds(chunk * CHUNK, CHUNK)
        parts = [B[x, half, own, :].reshape(CHUNK * ny, LANES) for half in range(2)]
        high, low = split(jnp.concatenate(parts, axis=1))
        der_z = dot(high, CZ[:, nz:]) + dot(low, CZ[:, nz:])
        for half in range(2):
            stiffness = K[xk, half]
            CO[0, xk, half] = C1 * stiffness * parts[half].reshape(CHUNK, ny, LANES)
            along = der_z[:, half * LANES : (half + 1) * LANES].reshape(CHUNK, ny, LANES)
            CO[3, xk, half] = (D1 * D1) * stiffness * along
        return 0

    lax.fori_loop(0, chunks, prepare, 0)

    def all_depths(level):
        def one(block, _):
            along_depth(levels[level], block, depth[(level + 1) % 2])
            return 0

        lax.fori_loop(0, nx // BLOCK, one, 0)

    all_depths(1)

    def coefficients(chunk):
        def plane(j, _):
            x = chunk * CHUNK + j
            for half in range(2):
                stiffness = (D1 * D1) * K[x, half]
                CO[1, x, half] = stiffness * slopes(0, WIDTH + x, half)
                CO[2, x, half] = stiffness * slopes(1, WIDTH + x, half)
            return 0

        lax.fori_loop(0, CHUNK, plane, 0)

    for i in (4, 5):
        loaded(i)

    def stencil(n, chunk, half):
        before, now, after = levels[n], levels[n + 1], levels[n + 2]
        x0 = chunk * CHUNK
        amplitudes = [
            jnp.where(source[0, 0] - gx * nx == x0 + j, wave[0, n], 0.0) for j in range(CHUNK)
        ]
        for top in range(0, ny, 8):
            tile = pl.ds(TOP + top, 8)
            row = pl.ds(top, 8)
            planes = [
                [now[field, x0 + k, half, tile, :] for k in range(CHUNK + 2 * WIDTH)]
                for field in range(2)
            ]
            for j in range(CHUNK):
                x = x0 + j
                co = [CO[i, x, half, row, :] for i in range(4)]
                for field in range(2):
                    xs = planes[field]
                    here = xs[WIDTH + j]
                    lap = (3.0 * second[0]) * here + depth[n % 2][field, 0, x, half, row, :]
                    der_x = der_y = None
                    for reach in range(1, WIDTH + 1):
                        xa, xb = xs[WIDTH + j + reach], xs[WIDTH + j - reach]
                        ya = now[field, x + WIDTH, half, pl.ds(TOP + top + reach, 8), :]
                        yb = now[field, x + WIDTH, half, pl.ds(TOP + top - reach, 8), :]
                        pairs = (xa + xb) + (ya + yb)
                        dx, dy = xa - xb, ya - yb
                        if reach == 1:
                            lap, der_x, der_y = lap + pairs, dx, dy
                        else:
                            lap = lap + second[reach] * pairs
                            der_x = der_x + first[reach - 1] * dx
                            der_y = der_y + first[reach - 1] * dy
                    change = co[0] * lap + co[1] * der_x + co[2] * der_y
                    change = change + co[3] * depth[n % 2][field, 1, x, half, row, :]
                    if field == 0:
                        change = change + amplitudes[j] * SM[half, row, :]
                        Q[n, x, half, row, :] = change
                    else:
                        change = change + R[n, x, half, row, :]
                    old = before[field, x + WIDTH, half, tile, :]
                    after[field, x + WIDTH, half, tile, :] = (2.0 * here - old) + change

    def send_on(level, chunk):
        def face(side, index):
            x_copy(level - 1, side, index).wait_send()
            x_copy(level, side, index).start()

        def strip(side, index):
            y_copy(level - 1, chunk, side, index).wait_send()
            y_copy(level, chunk, side, index).start()

        on_border(chunk, face)
        for_sides(sides_y, strip)

    def out_copies(x):
        for field, out in enumerate((fwd_out, adj_out)):
            for half in range(2):
                yield pltpu.make_async_copy(
                    F5.at[field, pl.ds(WIDTH + x.start, x.size), half, own, :],
                    out.at[0, x, :, pl.ds(half * LANES, LANES)],
                    out_sem.at[field, half],
                )

    def chosen(shot, owner, k):
        valid = (blocks[shot, 0, owner] == k) & (counts[shot, gy, owner] > 0)
        return jnp.where(valid, 1.0, 0.0)

    def imaging(chunk):
        for copy in out_copies(pl.ds(chunk * CHUNK, CHUNK)):
            copy.start()
        x0 = chunk * CHUNK
        for k in range(CHUNK // 2):
            for half in range(2):
                total = None
                for odd in range(2):
                    x = x0 + 2 * k + odd
                    for later in range(2, STEPS + 2):
                        term = levels[later][1, x + WIDTH, half, own, :] * Q[STEPS + 1 - later, x, half]
                        total = term if total is None else total + term
                TI[k, half] = total
        rows_k = []
        for k in range(CHUNK // 2):
            halves = [
                TI[k, half, pl.ds(0, ny // 2, stride=2), :] + TI[k, half, pl.ds(1, ny // 2, stride=2), :]
                for half in range(2)
            ]
            rows_k.append(jnp.concatenate(halves, axis=1))
        high, low = split(jnp.concatenate(rows_k, axis=0))
        coarse = dot(high, PZ[...]) + dot(low, PZ[...])
        row = None
        for k in range(CHUNK // 2):
            term = chosen(me, chunk, k) * coarse[k * (ny // 2) : (k + 1) * (ny // 2), :]
            row = term if row is None else row + term

        @pl.when(chunk == me)
        def _():
            INC[me] = row

        @pl.when(chunk != me)
        def _():
            OUTG[chunk] = row
            pltpu.make_async_remote_copy(
                src_ref=OUTG.at[chunk],
                dst_ref=INC.at[me],
                send_sem=g_send,
                recv_sem=g_recv,
                device_id={"shot": chunk},
                device_id_type=MESH,
            ).start()

    for copy in small[4:]:
        copy.wait()

    for n in range(STEPS):
        def run(i, _):
            chunk = order(i)
            await_halos(n + 1, chunk)
            if n == 0:
                coefficients(chunk)
            def part(half, _):
                stencil(n, chunk, half)
                return 0

            lax.fori_loop(0, 2, part, 0)
            if n < STEPS - 1:
                send_on(n + 2, chunk)
            else:
                imaging(chunk)
            return 0

        lax.fori_loop(0, chunks, run, 0)
        if n < STEPS - 1:
            all_depths(n + 2)

    others = pltpu.make_async_remote_copy(
        src_ref=OUTG.at[pl.ds(0, shots - 1)],
        dst_ref=INC.at[pl.ds(0, shots - 1)],
        send_sem=g_send,
        recv_sem=g_recv,
        device_id={"shot": lax.rem(me + 1, shots)},
        device_id_type=MESH,
    )
    others.wait_recv()
    for k in range(CHUNK // 2):
        total = None
        for shot in range(shots):
            term = chosen(shot, me, k) * INC[shot]
            total = term if total is None else total + term
        grad_out[0, k] = total

    others.wait_send()
    for copy in out_copies(pl.ds(0, nx)):
        copy.wait()

    def done(chunk, _):
        for_sides(sides_y, lambda side, index: y_copy(STEPS, chunk, side, index).wait_send())
        return 0

    lax.fori_loop(0, chunks, done, 0)
    for_sides(sides_x, lambda side, index: x_copy(STEPS, side, index).wait_send())


def hand_on(fwd, adj, grad, fwd_out, adj_out, grad_out, fwd_here, adj_here, grad_here, sems):
    pieces = 4
    size = fwd.shape[1] // pieces
    ways = [(grad, grad_here, grad_out)]
    for src, here, dst in ((fwd, fwd_here, fwd_out), (adj, adj_here, adj_out)):
        for p in range(pieces):
            x = pl.ds(p * size, size)
            ways.append((src.at[:, x], here.at[:, x], dst.at[:, x]))
    ways = [
        (pltpu.make_async_copy(src, here, sems.at[0, i]), pltpu.make_async_copy(here, dst, sems.at[1, i]))
        for i, (src, here, dst) in enumerate(ways)
    ]
    for arrive, _ in ways:
        arrive.start()
    for arrive, leave in ways:
        arrive.wait()
        leave.start()
    for _, leave in ways:
        leave.wait()


def body(
    stiffness, buoyancy, fwd_prev, fwd_now, adj_prev, adj_now, wavelet, source_cell, receiver_cell,
    traces, aperture_blocks, aperture_count,
):
    nx, ny, nz = stiffness.shape
    shots = lax.axis_size("shot")
    nrec = traces.shape[1]
    chunks = nx // CHUNK
    xe, ye = nx + 2 * WIDTH, ny + 2 * TOP
    f32, bf16, i32 = jnp.float32, jnp.bfloat16, jnp.int32
    hbm = pl.BlockSpec(memory_space=pltpu.HBM)
    vmem = pl.BlockSpec(memory_space=pltpu.VMEM)
    dma = pltpu.SemaphoreType.DMA
    receivers = jnp.transpose(receiver_cell, (2, 0, 1))
    by_step = jnp.transpose(traces, (0, 2, 1))
    lists = jnp.swapaxes(aperture_blocks, 3, 4)
    out_shape = (
        jax.ShapeDtypeStruct(fwd_now.shape, f32),
        jax.ShapeDtypeStruct(adj_now.shape, f32),
        jax.ShapeDtypeStruct((1, nx // 2 // shots, ny // 2, nz // 2), f32),
    )
    results = pl.pallas_call(
        kernel,
        out_shape=out_shape,
        in_specs=[hbm] * 12,
        out_specs=(pl.BlockSpec(memory_space=pl.ANY),) * 2 + (vmem,),
        scratch_shapes=[
            pltpu.VMEM((2, xe, 2, ye, LANES), f32),
            pltpu.VMEM((3, xe, 2, ye, LANES), f32),
            pltpu.VMEM((2, xe, 2, ye, LANES), f32),
            pltpu.VMEM((2, xe, 2, ye, LANES), f32),
            pltpu.VMEM((2, xe, 2, ye, LANES), f32),
            pltpu.VMEM((2, xe, 2, ye, LANES), f32),
            pltpu.VMEM((nx, 2, ny, LANES), f32),
            pltpu.VMEM((4, nx, 2, ny, LANES), f32),
            pltpu.VMEM((STEPS, nx, 2, ny, LANES), f32),
            pltpu.VMEM((STEPS, nx, 2, ny, LANES), f32),
            pltpu.VMEM((nx * ny, nrec), bf16),
            pltpu.VMEM((STEPS, nz, nrec), bf16),
            pltpu.VMEM((STEPS, nz, nrec), bf16),
            pltpu.VMEM((nz, 2 * nz), bf16),
            pltpu.VMEM((nz, nz // 2), bf16),
            pltpu.VMEM((2, 2, nx, 2, ny, LANES), f32),
            pltpu.VMEM((2, 2, nx, 2, ny, LANES), f32),
            pltpu.VMEM((2, ny, LANES), f32),
            pltpu.VMEM((CHUNK // 2, 2, ny, LANES), f32),
            pltpu.VMEM((shots, ny // 2, nz // 2), f32),
            pltpu.VMEM((shots, ny // 2, nz // 2), f32),
            pltpu.VMEM(receivers.shape, i32),
            pltpu.VMEM(by_step.shape, f32),
            pltpu.SMEM(wavelet.shape, f32),
            pltpu.SMEM(source_cell.shape, i32),
            pltpu.SMEM((shots,) + lists.shape[3:], i32),
            pltpu.SMEM((shots,) + aperture_count.shape[2:], i32),
            dma((12,)),
            dma((2,)),
            dma((2, 2)),
            dma((chunks, 2)),
            dma((2, chunks, 2)),
            dma((2, 2)),
            dma(()),
            dma(()),
        ],
        compiler_params=pltpu.CompilerParams(
            collective_id=0, has_side_effects=True, vmem_limit_bytes=60 << 20
        ),
        name="window",
    )(
        stiffness, buoyancy, fwd_prev, fwd_now, adj_prev, adj_now, wavelet, source_cell,
        receivers, by_step, lists, aperture_count,
    )
    return pl.pallas_call(
        hand_on,
        out_shape=out_shape,
        in_specs=[hbm] * 3,
        out_specs=(hbm,) * 3,
        scratch_shapes=[pltpu.VMEM(out.shape, f32) for out in out_shape] + [dma((2, 9))],
        name="hand_on",
    )(*results)


def solution(mesh):
    in_specs = (
        P("gx", "gy", None),
        P("gx", "gy", None),
        P("shot", "gx", "gy", None),
        P("shot", "gx", "gy", None),
        P("shot", "gx", "gy", None),
        P("shot", "gx", "gy", None),
        P("shot", None),
        P("shot", None),
        P("shot", None, None),
        P("shot", None, None),
        P(),
        P(),
    )
    out_specs = (
        P("shot", "gx", "gy", None),
        P("shot", "gx", "gy", None),
        P("gx", "shot", "gy", None),
    )
    return jax.shard_map(body, mesh=mesh, in_specs=in_specs, out_specs=out_specs, check_vma=False)
```

```python
import jax
import jax.numpy as jnp
from jax import lax
from jax.experimental import pallas as pl
from jax.experimental.pallas import tpu as pltpu
from jax.sharding import PartitionSpec as P

MESH = pl.DeviceIdType.MESH
STEPS = 4
WIDTH = 4
BLOCK = 24
CHUNK = 6
TOP = 8
LANES = 128

C1, D1 = 8.0 / 5.0, 4.0 / 5.0
second = tuple(c / C1 for c in (-205.0 / 72.0, 8.0 / 5.0, -1.0 / 5.0, 8.0 / 315.0, -1.0 / 560.0))
first = tuple(d / D1 for d in (4.0 / 5.0, -1.0 / 5.0, 4.0 / 105.0, -1.0 / 280.0))


def split(v):
    high = v.astype(jnp.bfloat16)
    return high, (v - high.astype(jnp.float32)).astype(jnp.bfloat16)


def dot(a, b):
    return jnp.dot(a, b, preferred_element_type=jnp.float32)


def dot_nt(a, b):
    return lax.dot_general(a, b, (((1,), (1,)), ((), ())), preferred_element_type=jnp.float32)


def kernel(
    stiff, buoy, fwd0, fwd1, adj0, adj1, wave_in, source_in, receiver_in, traces_in, blocks_in, counts_in,
    fwd_out, adj_out, grad_out,
    F0, F1, F2, F3, F4, F5, K, CO, R, Q, A, BH, BL, CZ, PZ, Z0, Z1, SM, TI, OUTG, INC,
    receiver, traces, wave, source, blocks, counts,
    load_sem, x_send, x_recv, y_send, y_recv, out_sem, g_send, g_recv,
):
    levels = (F0, F1, F2, F3, F4, F5)
    depth = (Z0, Z1)
    B = F1.at[2]
    nx, ny, nz = stiff.shape
    chunks = nx // CHUNK
    gx, gy, me = lax.axis_index("gx"), lax.axis_index("gy"), lax.axis_index("shot")
    last_x, last_y = lax.axis_size("gx") - 1, lax.axis_size("gy") - 1
    shots = lax.axis_size("shot")
    own = pl.ds(TOP, ny)
    inner = pl.ds(WIDTH, nx)
    sides_x = ((gx > 0, gx - 1), (gx < last_x, gx + 1))
    sides_y = ((gy > 0, gy - 1), (gy < last_y, gy + 1))

    def for_sides(sides, do):
        for side, (there, index) in enumerate(sides):
            @pl.when(there)
            def _():
                do(side, index)

    barrier = pltpu.get_barrier_semaphore()
    peers = shots - 1
    for axis, sides in (("gx", sides_x), ("gy", sides_y)):
        for there, index in sides:
            @pl.when(there)
            def _():
                pl.semaphore_signal(barrier, inc=1, device_id={axis: index}, device_id_type=MESH)
            peers = peers + jnp.where(there, 1, 0)

    def greet(step, _):
        pl.semaphore_signal(
            barrier, inc=1, device_id={"shot": lax.rem(me + step, shots)}, device_id_type=MESH
        )
        return 0

    lax.fori_loop(1, shots, greet, 0)

    small = [
        pltpu.make_async_copy(src, dst, load_sem.at[6 + i])
        for i, (src, dst) in enumerate(
            (
                (receiver_in, receiver),
                (traces_in, traces),
                (wave_in, wave),
                (source_in, source),
                (blocks_in.at[:, gx, gy], blocks),
                (counts_in.at[:, gx], counts),
            )
        )
    ]
    large = (
        (buoy, F1.at[2, inner, :, own, :]),
        (fwd1.at[0], F1.at[0, inner, :, own, :]),
        (adj1.at[0], F1.at[1, inner, :, own, :]),
        (stiff, K),
        (fwd0.at[0], F0.at[0, inner, :, own, :]),
        (adj0.at[0], F0.at[1, inner, :, own, :]),
    )

    def load(i):
        src, dst = large[i]
        for half in range(2):
            pltpu.make_async_copy(
                src.at[:, :, pl.ds(half * LANES, LANES)], dst.at[:, half], load_sem.at[i]
            ).start()

    def loaded(i):
        dst = large[i][1]
        pltpu.make_async_copy(dst, dst, load_sem.at[i]).wait()

    for copy in small[:4]:
        copy.start()
    for i in range(6):
        load(i)
    for copy in small[4:]:
        copy.start()

    for side, (there, _) in enumerate(sides_x):
        @pl.when(jnp.logical_not(there))
        def _():
            at = pl.ds(side * (nx + WIDTH), WIDTH)
            for ref in levels[1 : STEPS + 1]:
                for field in range(ref.shape[0]):
                    ref[field, at, :, own, :] = jnp.zeros((WIDTH, 2, ny, LANES), jnp.float32)
    for side, (there, _) in enumerate(sides_y):
        @pl.when(jnp.logical_not(there))
        def _():
            at = pl.ds(TOP - WIDTH + side * (ny + WIDTH), WIDTH)

            def clear(x, _):
                for ref in levels[1 : STEPS + 1]:
                    for field in range(ref.shape[0]):
                        ref[field, x, :, at, :] = jnp.zeros((2, WIDTH, LANES), jnp.float32)
                return 0

            lax.fori_loop(WIDTH, nx + WIDTH, clear, 0)

    def x_edge(side):
        return pl.ds(WIDTH + side * (nx - WIDTH), WIDTH), pl.ds((1 - side) * (nx + WIDTH), WIDTH)

    def y_edge(side):
        return (
            pl.ds(TOP + side * (ny - WIDTH), WIDTH),
            pl.ds(TOP - WIDTH + (1 - side) * (ny + WIDTH), WIDTH),
        )

    def x_copy(level, side, index, arrival=False):
        ref = levels[level]
        mine, theirs = x_edge(1 - side if arrival else side)
        return pltpu.make_async_remote_copy(
            src_ref=ref.at[:, theirs if arrival else mine, :, own, :],
            dst_ref=ref.at[:, theirs, :, own, :],
            send_sem=x_send.at[side],
            recv_sem=x_recv.at[level % 2, side if arrival else 1 - side],
            device_id={"gx": index},
            device_id_type=MESH,
        )

    def y_copy(level, chunk, side, index, arrival=False):
        ref = levels[level]
        mine, theirs = y_edge(1 - side if arrival else side)
        x = pl.ds(WIDTH + chunk * CHUNK, CHUNK)
        return pltpu.make_async_remote_copy(
            src_ref=ref.at[:, x, :, theirs if arrival else mine, :],
            dst_ref=ref.at[:, x, :, theirs, :],
            send_sem=y_send.at[chunk, side],
            recv_sem=y_recv.at[level % 2, chunk, side if arrival else 1 - side],
            device_id={"gy": index},
            device_id_type=MESH,
        )

    def order(i):
        return lax.rem(chunks - i, chunks)

    def on_border(chunk, do):
        for side, border in enumerate((0, chunks - 1)):
            there, index = sides_x[side]

            @pl.when((chunk == border) & there)
            def _():
                do(side, index)

    def await_halos(level, chunk):
        on_border(chunk, lambda side, index: x_copy(level, side, index, True).wait_recv())
        for_sides(sides_y, lambda side, index: y_copy(level, chunk, side, index, True).wait_recv())

    for i in range(3):
        loaded(i)
    pl.semaphore_wait(barrier, peers)
    for_sides(sides_x, lambda side, index: x_copy(1, side, index).start())

    def first_strips(i, _):
        for_sides(sides_y, lambda side, index: y_copy(1, order(i), side, index).start())
        return 0

    lax.fori_loop(0, chunks, first_strips, 0)

    diff = lax.broadcasted_iota(jnp.int32, (nz, nz), 0) - lax.broadcasted_iota(jnp.int32, (nz, nz), 1)
    lap = jnp.zeros((nz, nz), jnp.float32)
    der = jnp.zeros((nz, nz), jnp.float32)
    for reach in range(1, WIDTH + 1):
        lap = jnp.where(jnp.abs(diff) == reach, second[reach], lap)
        der = jnp.where(diff == reach, first[reach - 1], der)
        der = jnp.where(diff == -reach, -first[reach - 1], der)
    CZ[:, 0:nz] = lap.astype(jnp.bfloat16)
    CZ[:, nz:] = der.astype(jnp.bfloat16)
    fine = lax.broadcasted_iota(jnp.int32, (nz, nz // 2), 0)
    pair = lax.broadcasted_iota(jnp.int32, (nz, nz // 2), 1) * 2
    PZ[...] = jnp.where((fine == pair) | (fine == pair + 1), 0.125, 0.0).astype(jnp.bfloat16)

    for copy in small[:4]:
        copy.wait()

    for half in range(2):
        row = lax.broadcasted_iota(jnp.int32, (ny, LANES), 0) + gy * ny
        col = lax.broadcasted_iota(jnp.int32, (ny, LANES), 1) + half * LANES
        SM[half] = jnp.where((row == source[0, 1]) & (col == source[0, 2]), 1.0, 0.0)

    rec_x = receiver[0] - gx * nx
    rec_y = receiver[1] - gy * ny
    inside = (rec_x >= 0) & (rec_x < nx) & (rec_y >= 0) & (rec_y < ny)
    cell = jnp.where(inside, rec_x * ny + rec_y, -1)
    nrec = cell.shape[1]
    rows = 128

    def hot(g, _):
        at = lax.broadcasted_iota(jnp.int32, (rows, nrec), 0) + g * rows
        A[pl.ds(pl.multiple_of(g * rows, rows), rows), :] = jnp.where(at == cell, 1.0, 0.0).astype(
            jnp.bfloat16
        )
        return 0

    lax.fori_loop(0, nx * ny // rows, hot, 0)
    rec_z = receiver[2]
    for n in range(STEPS):
        def place(g, _):
            at = lax.broadcasted_iota(jnp.int32, (64, nrec), 0) + g * 64
            high, low = split(jnp.where(at == rec_z, traces[0, n : n + 1, :], 0.0))
            where = pl.ds(pl.multiple_of(g * 64, 64), 64)
            BH[n, where, :] = high
            BL[n, where, :] = low
            return 0

        lax.fori_loop(0, nz // 64, place, 0)

    def inject(n, _):
        for part in range(2):
            hots = A[pl.ds(part * nx * ny // 2, nx * ny // 2), :]
            field = dot_nt(hots, BH[n]) + dot_nt(hots, BL[n])
            field = field.reshape(nx // 2, ny, nz)
            for half in range(2):
                R[n, pl.ds(part * nx // 2, nx // 2), half] = field[:, :, half * LANES : (half + 1) * LANES]
        return 0

    lax.fori_loop(0, STEPS, inject, 0)

    def along_depth(ref, block, out_ref):
        x = pl.ds(WIDTH + block * BLOCK, BLOCK)
        cells = BLOCK * ny
        parts = [
            jnp.concatenate(
                [ref[field, x, half, own, :].reshape(cells, LANES) for half in range(2)], axis=1
            )
            for field in range(2)
        ]
        high, low = split(jnp.concatenate(parts, axis=0))
        out = dot(high, CZ[...]) + dot(low, CZ[...])
        for field in range(2):
            for kind in range(2):
                for half in range(2):
                    at = kind * nz + half * LANES
                    piece = out[field * cells : (field + 1) * cells, at : at + LANES]
                    out_ref[field, kind, pl.ds(block * BLOCK, BLOCK), half] = piece.reshape(
                        BLOCK, ny, LANES
                    )

    def slopes(along, x, half):
        total = None
        for reach in range(1, WIDTH + 1):
            if along == 0:
                ahead, behind = B[x + reach, half, own, :], B[x - reach, half, own, :]
            else:
                ahead = B[x, half, pl.ds(TOP + reach, ny), :]
                behind = B[x, half, pl.ds(TOP - reach, ny), :]
            term = ahead - behind
            if reach > 1:
                term = first[reach - 1] * term
            total = term if total is None else total + term
        return total

    loaded(3)

    def prepare(block, _):
        x = pl.ds(WIDTH + block * BLOCK, BLOCK)
        xk = pl.ds(block * BLOCK, BLOCK)
        parts = [B[x, half, own, :].reshape(BLOCK * ny, LANES) for half in range(2)]
        high, low = split(jnp.concatenate(parts, axis=1))
        der_z = dot(high, CZ[:, nz:]) + dot(low, CZ[:, nz:])
        for half in range(2):
            stiffness = K[xk, half]
            CO[0, xk, half] = C1 * stiffness * parts[half].reshape(BLOCK, ny, LANES)
            along = der_z[:, half * LANES : (half + 1) * LANES].reshape(BLOCK, ny, LANES)
            CO[3, xk, half] = (D1 * D1) * stiffness * along
        return 0

    lax.fori_loop(0, nx // BLOCK, prepare, 0)

    def all_depths(level):
        def one(block, _):
            along_depth(levels[level], block, depth[(level + 1) % 2])
            return 0

        lax.fori_loop(0, nx // BLOCK, one, 0)

    all_depths(1)

    def coefficients(chunk):
        def plane(j, _):
            x = chunk * CHUNK + j
            for half in range(2):
                stiffness = (D1 * D1) * K[x, half]
                CO[1, x, half] = stiffness * slopes(0, WIDTH + x, half)
                CO[2, x, half] = stiffness * slopes(1, WIDTH + x, half)
            return 0

        lax.fori_loop(0, CHUNK, plane, 0)

    for i in (4, 5):
        loaded(i)

    def stencil(n, chunk, half):
        before, now, after = levels[n], levels[n + 1], levels[n + 2]
        x0 = chunk * CHUNK
        amplitudes = [
            jnp.where(source[0, 0] - gx * nx == x0 + j, wave[0, n], 0.0) for j in range(CHUNK)
        ]
        for top in range(0, ny, 8):
            tile = pl.ds(TOP + top, 8)
            row = pl.ds(top, 8)
            planes = [
                [now[field, x0 + k, half, tile, :] for k in range(CHUNK + 2 * WIDTH)]
                for field in range(2)
            ]
            for j in range(CHUNK):
                x = x0 + j
                co = [CO[i, x, half, row, :] for i in range(4)]
                for field in range(2):
                    xs = planes[field]
                    here = xs[WIDTH + j]
                    lap = (3.0 * second[0]) * here + depth[n % 2][field, 0, x, half, row, :]
                    der_x = der_y = None
                    for reach in range(1, WIDTH + 1):
                        xa, xb = xs[WIDTH + j + reach], xs[WIDTH + j - reach]
                        ya = now[field, x + WIDTH, half, pl.ds(TOP + top + reach, 8), :]
                        yb = now[field, x + WIDTH, half, pl.ds(TOP + top - reach, 8), :]
                        pairs = (xa + xb) + (ya + yb)
                        dx, dy = xa - xb, ya - yb
                        if reach == 1:
                            lap, der_x, der_y = lap + pairs, dx, dy
                        else:
                            lap = lap + second[reach] * pairs
                            der_x = der_x + first[reach - 1] * dx
                            der_y = der_y + first[reach - 1] * dy
                    change = co[0] * lap + co[1] * der_x + co[2] * der_y
                    change = change + co[3] * depth[n % 2][field, 1, x, half, row, :]
                    if field == 0:
                        change = change + amplitudes[j] * SM[half, row, :]
                        Q[n, x, half, row, :] = change
                    else:
                        change = change + R[n, x, half, row, :]
                    old = before[field, x + WIDTH, half, tile, :]
                    after[field, x + WIDTH, half, tile, :] = (2.0 * here - old) + change

    def send_on(level, chunk):
        def face(side, index):
            x_copy(level - 1, side, index).wait_send()
            x_copy(level, side, index).start()

        def strip(side, index):
            y_copy(level - 1, chunk, side, index).wait_send()
            y_copy(level, chunk, side, index).start()

        on_border(chunk, face)
        for_sides(sides_y, strip)

    def out_copies():
        for field, out in enumerate((fwd_out, adj_out)):
            for half in range(2):
                yield pltpu.make_async_copy(
                    F5.at[field, inner, half, own, :],
                    out.at[0, :, :, pl.ds(half * LANES, LANES)],
                    out_sem.at[field, half],
                )

    def chosen(shot, owner, k):
        valid = (blocks[shot, 0, owner] == k) & (counts[shot, gy, owner] > 0)
        return jnp.where(valid, 1.0, 0.0)

    def imaging(chunk):
        x0 = chunk * CHUNK
        for k in range(CHUNK // 2):
            for half in range(2):
                total = None
                for odd in range(2):
                    x = x0 + 2 * k + odd
                    for later in range(2, STEPS + 2):
                        term = levels[later][1, x + WIDTH, half, own, :] * Q[STEPS + 1 - later, x, half]
                        total = term if total is None else total + term
                TI[k, half] = total
        rows_k = []
        for k in range(CHUNK // 2):
            halves = [
                TI[k, half, pl.ds(0, ny // 2, stride=2), :] + TI[k, half, pl.ds(1, ny // 2, stride=2), :]
                for half in range(2)
            ]
            rows_k.append(jnp.concatenate(halves, axis=1))
        high, low = split(jnp.concatenate(rows_k, axis=0))
        coarse = dot(high, PZ[...]) + dot(low, PZ[...])
        row = None
        for k in range(CHUNK // 2):
            term = chosen(me, chunk, k) * coarse[k * (ny // 2) : (k + 1) * (ny // 2), :]
            row = term if row is None else row + term

        @pl.when(chunk == me)
        def _():
            INC[me] = row

        @pl.when(chunk != me)
        def _():
            OUTG[chunk] = row
            pltpu.make_async_remote_copy(
                src_ref=OUTG.at[chunk],
                dst_ref=INC.at[me],
                send_sem=g_send,
                recv_sem=g_recv,
                device_id={"shot": chunk},
                device_id_type=MESH,
            ).start()

    for copy in small[4:]:
        copy.wait()

    for n in range(STEPS):
        def run(i, _):
            chunk = order(i)
            await_halos(n + 1, chunk)
            if n == 0:
                coefficients(chunk)
            for half in range(2):
                stencil(n, chunk, half)
            if n < STEPS - 1:
                send_on(n + 2, chunk)
            else:
                imaging(chunk)
            return 0

        lax.fori_loop(0, chunks, run, 0)
        if n < STEPS - 1:
            all_depths(n + 2)

    for copy in out_copies():
        copy.start()
    weights = [[chosen(shot, me, k) for shot in range(shots)] for k in range(CHUNK // 2)]

    def done(chunk, _):
        for_sides(sides_y, lambda side, index: y_copy(STEPS, chunk, side, index).wait_send())
        return 0

    lax.fori_loop(0, chunks, done, 0)
    for_sides(sides_x, lambda side, index: x_copy(STEPS, side, index).wait_send())

    others = pltpu.make_async_remote_copy(
        src_ref=OUTG.at[pl.ds(0, shots - 1)],
        dst_ref=INC.at[pl.ds(0, shots - 1)],
        send_sem=g_send,
        recv_sem=g_recv,
        device_id={"shot": lax.rem(me + 1, shots)},
        device_id_type=MESH,
    )
    others.wait_send()
    for copy in out_copies():
        copy.wait()
    others.wait_recv()
    for k in range(CHUNK // 2):
        total = None
        for shot in range(shots):
            term = weights[k][shot] * INC[shot]
            total = term if total is None else total + term
        grad_out[0, k] = total


def hand_on(fwd, adj, grad, fwd_out, adj_out, grad_out, fwd_here, adj_here, grad_here, sems):
    pieces = 4
    size = fwd.shape[1] // pieces
    ways = [(grad, grad_here, grad_out)]
    for src, here, dst in ((fwd, fwd_here, fwd_out), (adj, adj_here, adj_out)):
        for p in range(pieces):
            x = pl.ds(p * size, size)
            ways.append((src.at[:, x], here.at[:, x], dst.at[:, x]))
    ways = [
        (pltpu.make_async_copy(src, here, sems.at[0, i]), pltpu.make_async_copy(here, dst, sems.at[1, i]))
        for i, (src, here, dst) in enumerate(ways)
    ]
    for arrive, _ in ways:
        arrive.start()
    for arrive, leave in ways:
        arrive.wait()
        leave.start()
    for _, leave in ways:
        leave.wait()


def body(
    stiffness, buoyancy, fwd_prev, fwd_now, adj_prev, adj_now, wavelet, source_cell, receiver_cell,
    traces, aperture_blocks, aperture_count,
):
    nx, ny, nz = stiffness.shape
    shots = lax.axis_size("shot")
    nrec = traces.shape[1]
    chunks = nx // CHUNK
    xe, ye = nx + 2 * WIDTH, ny + 2 * TOP
    f32, bf16, i32 = jnp.float32, jnp.bfloat16, jnp.int32
    hbm = pl.BlockSpec(memory_space=pltpu.HBM)
    vmem = pl.BlockSpec(memory_space=pltpu.VMEM)
    dma = pltpu.SemaphoreType.DMA
    receivers = jnp.transpose(receiver_cell, (2, 0, 1))
    by_step = jnp.transpose(traces, (0, 2, 1))
    lists = jnp.swapaxes(aperture_blocks, 3, 4)
    out_shape = (
        jax.ShapeDtypeStruct(fwd_now.shape, f32),
        jax.ShapeDtypeStruct(adj_now.shape, f32),
        jax.ShapeDtypeStruct((1, nx // 2 // shots, ny // 2, nz // 2), f32),
    )
    results = pl.pallas_call(
        kernel,
        out_shape=out_shape,
        in_specs=[hbm] * 12,
        out_specs=(pl.BlockSpec(memory_space=pl.ANY),) * 2 + (vmem,),
        scratch_shapes=[
            pltpu.VMEM((2, xe, 2, ye, LANES), f32),
            pltpu.VMEM((3, xe, 2, ye, LANES), f32),
            pltpu.VMEM((2, xe, 2, ye, LANES), f32),
            pltpu.VMEM((2, xe, 2, ye, LANES), f32),
            pltpu.VMEM((2, xe, 2, ye, LANES), f32),
            pltpu.VMEM((2, xe, 2, ye, LANES), f32),
            pltpu.VMEM((nx, 2, ny, LANES), f32),
            pltpu.VMEM((4, nx, 2, ny, LANES), f32),
            pltpu.VMEM((STEPS, nx, 2, ny, LANES), f32),
            pltpu.VMEM((STEPS, nx, 2, ny, LANES), f32),
            pltpu.VMEM((nx * ny, nrec), bf16),
            pltpu.VMEM((STEPS, nz, nrec), bf16),
            pltpu.VMEM((STEPS, nz, nrec), bf16),
            pltpu.VMEM((nz, 2 * nz), bf16),
            pltpu.VMEM((nz, nz // 2), bf16),
            pltpu.VMEM((2, 2, nx, 2, ny, LANES), f32),
            pltpu.VMEM((2, 2, nx, 2, ny, LANES), f32),
            pltpu.VMEM((2, ny, LANES), f32),
            pltpu.VMEM((CHUNK // 2, 2, ny, LANES), f32),
            pltpu.VMEM((shots, ny // 2, nz // 2), f32),
            pltpu.VMEM((shots, ny // 2, nz // 2), f32),
            pltpu.VMEM(receivers.shape, i32),
            pltpu.VMEM(by_step.shape, f32),
            pltpu.SMEM(wavelet.shape, f32),
            pltpu.SMEM(source_cell.shape, i32),
            pltpu.SMEM((shots,) + lists.shape[3:], i32),
            pltpu.SMEM((shots,) + aperture_count.shape[2:], i32),
            dma((12,)),
            dma((2,)),
            dma((2, 2)),
            dma((chunks, 2)),
            dma((2, chunks, 2)),
            dma((2, 2)),
            dma(()),
            dma(()),
        ],
        compiler_params=pltpu.CompilerParams(
            collective_id=0, has_side_effects=True, vmem_limit_bytes=60 << 20
        ),
        name="window",
    )(
        stiffness, buoyancy, fwd_prev, fwd_now, adj_prev, adj_now, wavelet, source_cell,
        receivers, by_step, lists, aperture_count,
    )
    return pl.pallas_call(
        hand_on,
        out_shape=out_shape,
        in_specs=[hbm] * 3,
        out_specs=(hbm,) * 3,
        scratch_shapes=[pltpu.VMEM(out.shape, f32) for out in out_shape] + [dma((2, 9))],
        name="hand_on",
    )(*results)


def solution(mesh):
    in_specs = (
        P("gx", "gy", None),
        P("gx", "gy", None),
        P("shot", "gx", "gy", None),
        P("shot", "gx", "gy", None),
        P("shot", "gx", "gy", None),
        P("shot", "gx", "gy", None),
        P("shot", None),
        P("shot", None),
        P("shot", None, None),
        P("shot", None, None),
        P(),
        P(),
    )
    out_specs = (
        P("shot", "gx", "gy", None),
        P("shot", "gx", "gy", None),
        P("gx", "shot", "gy", None),
    )
    return jax.shard_map(body, mesh=mesh, in_specs=in_specs, out_specs=out_specs, check_vma=False)
```

```python
import jax
import jax.numpy as jnp
from jax import lax
from jax.experimental import pallas as pl
from jax.experimental.pallas import tpu as pltpu
from jax.sharding import PartitionSpec as P

MESH = pl.DeviceIdType.MESH
STEPS = 4
WIDTH = 4
BLOCK = 48
CHUNK = 6
TOP = 8
LANES = 128

C1, D1 = 8.0 / 5.0, 4.0 / 5.0
second = tuple(c / C1 for c in (-205.0 / 72.0, 8.0 / 5.0, -1.0 / 5.0, 8.0 / 315.0, -1.0 / 560.0))
first = tuple(d / D1 for d in (4.0 / 5.0, -1.0 / 5.0, 4.0 / 105.0, -1.0 / 280.0))


def split(v):
    high = v.astype(jnp.bfloat16)
    return high, (v - high.astype(jnp.float32)).astype(jnp.bfloat16)


def dot(a, b):
    return jnp.dot(a, b, preferred_element_type=jnp.float32)


def dot_nt(a, b):
    return lax.dot_general(a, b, (((1,), (1,)), ((), ())), preferred_element_type=jnp.float32)


def kernel(
    stiff, buoy, fwd0, fwd1, adj0, adj1, wave_in, source_in, receiver_in, traces_in, blocks_in, counts_in,
    fwd_out, adj_out, grad_out,
    F0, F1, F2, F3, F4, F5, K, CO, R, Q, A, BH, BL, CZ, PZ, Z0, Z1, SM, TI, OUTG, INC,
    receiver, traces, wave, source, blocks, counts,
    load_sem, x_send, x_recv, y_send, y_recv, out_sem, g_send, g_recv,
):
    levels = (F0, F1, F2, F3, F4, F5)
    depth = (Z0, Z1)
    B = F1.at[2]
    nx, ny, nz = stiff.shape
    chunks = nx // CHUNK
    gx, gy, me = lax.axis_index("gx"), lax.axis_index("gy"), lax.axis_index("shot")
    last_x, last_y = lax.axis_size("gx") - 1, lax.axis_size("gy") - 1
    shots = lax.axis_size("shot")
    own = pl.ds(TOP, ny)
    inner = pl.ds(WIDTH, nx)
    sides_x = ((gx > 0, gx - 1), (gx < last_x, gx + 1))
    sides_y = ((gy > 0, gy - 1), (gy < last_y, gy + 1))

    def for_sides(sides, do):
        for side, (there, index) in enumerate(sides):
            @pl.when(there)
            def _():
                do(side, index)

    barrier = pltpu.get_barrier_semaphore()
    peers = shots - 1
    for axis, sides in (("gx", sides_x), ("gy", sides_y)):
        for there, index in sides:
            @pl.when(there)
            def _():
                pl.semaphore_signal(barrier, inc=1, device_id={axis: index}, device_id_type=MESH)
            peers = peers + jnp.where(there, 1, 0)

    def greet(step, _):
        pl.semaphore_signal(
            barrier, inc=1, device_id={"shot": lax.rem(me + step, shots)}, device_id_type=MESH
        )
        return 0

    lax.fori_loop(1, shots, greet, 0)

    small = [
        pltpu.make_async_copy(src, dst, load_sem.at[6 + i])
        for i, (src, dst) in enumerate(
            (
                (receiver_in, receiver),
                (traces_in, traces),
                (wave_in, wave),
                (source_in, source),
                (blocks_in.at[:, gx, gy], blocks),
                (counts_in.at[:, gx], counts),
            )
        )
    ]
    large = (
        (buoy, F1.at[2, inner, :, own, :]),
        (fwd1.at[0], F1.at[0, inner, :, own, :]),
        (adj1.at[0], F1.at[1, inner, :, own, :]),
        (stiff, K),
        (fwd0.at[0], F0.at[0, inner, :, own, :]),
        (adj0.at[0], F0.at[1, inner, :, own, :]),
    )

    def load(i):
        src, dst = large[i]
        for half in range(2):
            pltpu.make_async_copy(
                src.at[:, :, pl.ds(half * LANES, LANES)], dst.at[:, half], load_sem.at[i]
            ).start()

    def loaded(i):
        dst = large[i][1]
        pltpu.make_async_copy(dst, dst, load_sem.at[i]).wait()

    for copy in small[:4]:
        copy.start()
    for i in range(6):
        load(i)
    for copy in small[4:]:
        copy.start()

    for side, (there, _) in enumerate(sides_x):
        @pl.when(jnp.logical_not(there))
        def _():
            at = pl.ds(side * (nx + WIDTH), WIDTH)
            for ref in levels[1 : STEPS + 1]:
                for field in range(ref.shape[0]):
                    ref[field, at, :, own, :] = jnp.zeros((WIDTH, 2, ny, LANES), jnp.float32)
    for side, (there, _) in enumerate(sides_y):
        @pl.when(jnp.logical_not(there))
        def _():
            at = pl.ds(TOP - WIDTH + side * (ny + WIDTH), WIDTH)

            def clear(x, _):
                for ref in levels[1 : STEPS + 1]:
                    for field in range(ref.shape[0]):
                        ref[field, x, :, at, :] = jnp.zeros((2, WIDTH, LANES), jnp.float32)
                return 0

            lax.fori_loop(WIDTH, nx + WIDTH, clear, 0)

    def x_edge(side):
        return pl.ds(WIDTH + side * (nx - WIDTH), WIDTH), pl.ds((1 - side) * (nx + WIDTH), WIDTH)

    def y_edge(side):
        return (
            pl.ds(TOP + side * (ny - WIDTH), WIDTH),
            pl.ds(TOP - WIDTH + (1 - side) * (ny + WIDTH), WIDTH),
        )

    def x_copy(level, side, index, arrival=False):
        ref = levels[level]
        mine, theirs = x_edge(1 - side if arrival else side)
        return pltpu.make_async_remote_copy(
            src_ref=ref.at[:, theirs if arrival else mine, :, own, :],
            dst_ref=ref.at[:, theirs, :, own, :],
            send_sem=x_send.at[side],
            recv_sem=x_recv.at[level % 2, side if arrival else 1 - side],
            device_id={"gx": index},
            device_id_type=MESH,
        )

    def y_copy(level, chunk, side, index, arrival=False):
        ref = levels[level]
        mine, theirs = y_edge(1 - side if arrival else side)
        x = pl.ds(WIDTH + chunk * CHUNK, CHUNK)
        return pltpu.make_async_remote_copy(
            src_ref=ref.at[:, x, :, theirs if arrival else mine, :],
            dst_ref=ref.at[:, x, :, theirs, :],
            send_sem=y_send.at[chunk, side],
            recv_sem=y_recv.at[level % 2, chunk, side if arrival else 1 - side],
            device_id={"gy": index},
            device_id_type=MESH,
        )

    def order(i):
        return lax.rem(chunks - i, chunks)

    def on_border(chunk, do):
        for side, border in enumerate((0, chunks - 1)):
            there, index = sides_x[side]

            @pl.when((chunk == border) & there)
            def _():
                do(side, index)

    def await_halos(level, chunk):
        on_border(chunk, lambda side, index: x_copy(level, side, index, True).wait_recv())
        for_sides(sides_y, lambda side, index: y_copy(level, chunk, side, index, True).wait_recv())

    for i in range(3):
        loaded(i)
    pl.semaphore_wait(barrier, peers)
    for_sides(sides_x, lambda side, index: x_copy(1, side, index).start())

    def first_strips(i, _):
        for_sides(sides_y, lambda side, index: y_copy(1, order(i), side, index).start())
        return 0

    lax.fori_loop(0, chunks, first_strips, 0)

    diff = lax.broadcasted_iota(jnp.int32, (nz, nz), 0) - lax.broadcasted_iota(jnp.int32, (nz, nz), 1)
    lap = jnp.zeros((nz, nz), jnp.float32)
    der = jnp.zeros((nz, nz), jnp.float32)
    for reach in range(1, WIDTH + 1):
        lap = jnp.where(jnp.abs(diff) == reach, second[reach], lap)
        der = jnp.where(diff == reach, first[reach - 1], der)
        der = jnp.where(diff == -reach, -first[reach - 1], der)
    CZ[:, 0:nz] = lap.astype(jnp.bfloat16)
    CZ[:, nz:] = der.astype(jnp.bfloat16)
    fine = lax.broadcasted_iota(jnp.int32, (nz, nz // 2), 0)
    pair = lax.broadcasted_iota(jnp.int32, (nz, nz // 2), 1) * 2
    PZ[...] = jnp.where((fine == pair) | (fine == pair + 1), 0.125, 0.0).astype(jnp.bfloat16)

    for copy in small[:4]:
        copy.wait()

    for half in range(2):
        row = lax.broadcasted_iota(jnp.int32, (ny, LANES), 0) + gy * ny
        col = lax.broadcasted_iota(jnp.int32, (ny, LANES), 1) + half * LANES
        SM[half] = jnp.where((row == source[0, 1]) & (col == source[0, 2]), 1.0, 0.0)

    rec_x = receiver[0] - gx * nx
    rec_y = receiver[1] - gy * ny
    inside = (rec_x >= 0) & (rec_x < nx) & (rec_y >= 0) & (rec_y < ny)
    cell = jnp.where(inside, rec_x * ny + rec_y, -1)
    nrec = cell.shape[1]
    rows = 128

    def hot(g, _):
        at = lax.broadcasted_iota(jnp.int32, (rows, nrec), 0) + g * rows
        A[pl.ds(pl.multiple_of(g * rows, rows), rows), :] = jnp.where(at == cell, 1.0, 0.0).astype(
            jnp.bfloat16
        )
        return 0

    lax.fori_loop(0, nx * ny // rows, hot, 0)
    rec_z = receiver[2]
    for n in range(STEPS):
        def place(g, _):
            at = lax.broadcasted_iota(jnp.int32, (64, nrec), 0) + g * 64
            high, low = split(jnp.where(at == rec_z, traces[0, n : n + 1, :], 0.0))
            where = pl.ds(pl.multiple_of(g * 64, 64), 64)
            BH[n, where, :] = high
            BL[n, where, :] = low
            return 0

        lax.fori_loop(0, nz // 64, place, 0)

    def inject(n, _):
        for part in range(2):
            hots = A[pl.ds(part * nx * ny // 2, nx * ny // 2), :]
            field = dot_nt(hots, BH[n]) + dot_nt(hots, BL[n])
            field = field.reshape(nx // 2, ny, nz)
            for half in range(2):
                R[n, pl.ds(part * nx // 2, nx // 2), half] = field[:, :, half * LANES : (half + 1) * LANES]
        return 0

    lax.fori_loop(0, STEPS, inject, 0)

    def along_depth(ref, block, out_ref):
        x = pl.ds(WIDTH + block * BLOCK, BLOCK)
        cells = BLOCK * ny
        parts = [
            jnp.concatenate(
                [ref[field, x, half, own, :].reshape(cells, LANES) for half in range(2)], axis=1
            )
            for field in range(2)
        ]
        high, low = split(jnp.concatenate(parts, axis=0))
        out = dot(high, CZ[...]) + dot(low, CZ[...])
        for field in range(2):
            for kind in range(2):
                for half in range(2):
                    at = kind * nz + half * LANES
                    piece = out[field * cells : (field + 1) * cells, at : at + LANES]
                    out_ref[field, kind, pl.ds(block * BLOCK, BLOCK), half] = piece.reshape(
                        BLOCK, ny, LANES
                    )

    def slopes(along, x, half):
        total = None
        for reach in range(1, WIDTH + 1):
            if along == 0:
                ahead, behind = B[x + reach, half, own, :], B[x - reach, half, own, :]
            else:
                ahead = B[x, half, pl.ds(TOP + reach, ny), :]
                behind = B[x, half, pl.ds(TOP - reach, ny), :]
            term = ahead - behind
            if reach > 1:
                term = first[reach - 1] * term
            total = term if total is None else total + term
        return total

    loaded(3)

    def prepare(block, _):
        x = pl.ds(WIDTH + block * BLOCK, BLOCK)
        xk = pl.ds(block * BLOCK, BLOCK)
        parts = [B[x, half, own, :].reshape(BLOCK * ny, LANES) for half in range(2)]
        high, low = split(jnp.concatenate(parts, axis=1))
        der_z = dot(high, CZ[:, nz:]) + dot(low, CZ[:, nz:])
        for half in range(2):
            stiffness = K[xk, half]
            CO[0, xk, half] = C1 * stiffness * parts[half].reshape(BLOCK, ny, LANES)
            along = der_z[:, half * LANES : (half + 1) * LANES].reshape(BLOCK, ny, LANES)
            CO[3, xk, half] = (D1 * D1) * stiffness * along
        return 0

    lax.fori_loop(0, nx // BLOCK, prepare, 0)

    def all_depths(level):
        def one(block, _):
            along_depth(levels[level], block, depth[(level + 1) % 2])
            return 0

        lax.fori_loop(0, nx // BLOCK, one, 0)

    all_depths(1)

    def coefficients(chunk):
        def plane(j, _):
            x = chunk * CHUNK + j
            for half in range(2):
                stiffness = (D1 * D1) * K[x, half]
                CO[1, x, half] = stiffness * slopes(0, WIDTH + x, half)
                CO[2, x, half] = stiffness * slopes(1, WIDTH + x, half)
            return 0

        lax.fori_loop(0, CHUNK, plane, 0)

    for i in (4, 5):
        loaded(i)

    def stencil(n, chunk, half):
        before, now, after = levels[n], levels[n + 1], levels[n + 2]
        x0 = chunk * CHUNK
        amplitudes = [
            jnp.where(source[0, 0] - gx * nx == x0 + j, wave[0, n], 0.0) for j in range(CHUNK)
        ]
        for top in range(0, ny, 8):
            tile = pl.ds(TOP + top, 8)
            row = pl.ds(top, 8)
            planes = [
                [now[field, x0 + k, half, tile, :] for k in range(CHUNK + 2 * WIDTH)]
                for field in range(2)
            ]
            for j in range(CHUNK):
                x = x0 + j
                co = [CO[i, x, half, row, :] for i in range(4)]
                for field in range(2):
                    xs = planes[field]
                    here = xs[WIDTH + j]
                    lap = (3.0 * second[0]) * here + depth[n % 2][field, 0, x, half, row, :]
                    der_x = der_y = None
                    for reach in range(1, WIDTH + 1):
                        xa, xb = xs[WIDTH + j + reach], xs[WIDTH + j - reach]
                        ya = now[field, x + WIDTH, half, pl.ds(TOP + top + reach, 8), :]
                        yb = now[field, x + WIDTH, half, pl.ds(TOP + top - reach, 8), :]
                        pairs = (xa + xb) + (ya + yb)
                        dx, dy = xa - xb, ya - yb
                        if reach == 1:
                            lap, der_x, der_y = lap + pairs, dx, dy
                        else:
                            lap = lap + second[reach] * pairs
                            der_x = der_x + first[reach - 1] * dx
                            der_y = der_y + first[reach - 1] * dy
                    change = co[0] * lap + co[1] * der_x + co[2] * der_y
                    change = change + co[3] * depth[n % 2][field, 1, x, half, row, :]
                    if field == 0:
                        change = change + amplitudes[j] * SM[half, row, :]
                        Q[n, x, half, row, :] = change
                    else:
                        change = change + R[n, x, half, row, :]
                    old = before[field, x + WIDTH, half, tile, :]
                    after[field, x + WIDTH, half, tile, :] = (2.0 * here - old) + change

    def send_on(level, chunk):
        def face(side, index):
            x_copy(level - 1, side, index).wait_send()
            x_copy(level, side, index).start()

        def strip(side, index):
            y_copy(level - 1, chunk, side, index).wait_send()
            y_copy(level, chunk, side, index).start()

        on_border(chunk, face)
        for_sides(sides_y, strip)

    def out_copies():
        for field, out in enumerate((fwd_out, adj_out)):
            for half in range(2):
                yield pltpu.make_async_copy(
                    F5.at[field, inner, half, own, :],
                    out.at[0, :, :, pl.ds(half * LANES, LANES)],
                    out_sem.at[field, half],
                )

    def chosen(shot, owner, k):
        valid = (blocks[shot, 0, owner] == k) & (counts[shot, gy, owner] > 0)
        return jnp.where(valid, 1.0, 0.0)

    def imaging(chunk):
        x0 = chunk * CHUNK
        for k in range(CHUNK // 2):
            for half in range(2):
                total = None
                for odd in range(2):
                    x = x0 + 2 * k + odd
                    for later in range(2, STEPS + 2):
                        term = levels[later][1, x + WIDTH, half, own, :] * Q[STEPS + 1 - later, x, half]
                        total = term if total is None else total + term
                TI[k, half] = total
        rows_k = []
        for k in range(CHUNK // 2):
            halves = [
                TI[k, half, pl.ds(0, ny // 2, stride=2), :] + TI[k, half, pl.ds(1, ny // 2, stride=2), :]
                for half in range(2)
            ]
            rows_k.append(jnp.concatenate(halves, axis=1))
        high, low = split(jnp.concatenate(rows_k, axis=0))
        coarse = dot(high, PZ[...]) + dot(low, PZ[...])
        row = None
        for k in range(CHUNK // 2):
            term = chosen(me, chunk, k) * coarse[k * (ny // 2) : (k + 1) * (ny // 2), :]
            row = term if row is None else row + term
        return row

    def deliver(chunk, row):
        @pl.when(chunk == me)
        def _():
            INC[me] = row

        @pl.when(chunk != me)
        def _():
            OUTG[chunk] = row
            pltpu.make_async_remote_copy(
                src_ref=OUTG.at[chunk],
                dst_ref=INC.at[me],
                send_sem=g_send,
                recv_sem=g_recv,
                device_id={"shot": chunk},
                device_id_type=MESH,
            ).start()

    for copy in small[4:]:
        copy.wait()

    for n in range(STEPS):
        def run(i, _):
            chunk = order(i)
            await_halos(n + 1, chunk)
            if n == 0:
                coefficients(chunk)
            if n == STEPS - 1:
                earlier = order(lax.rem(i + chunks - 1, chunks))
                row = imaging(earlier)
            for half in range(2):
                stencil(n, chunk, half)
            if n < STEPS - 1:
                send_on(n + 2, chunk)
            else:
                @pl.when(i > 0)
                def _():
                    deliver(earlier, row)
            return 0

        lax.fori_loop(0, chunks, run, 0)
        if n < STEPS - 1:
            all_depths(n + 2)
        else:
            deliver(order(chunks - 1), imaging(order(chunks - 1)))

    for copy in out_copies():
        copy.start()
    weights = [[chosen(shot, me, k) for shot in range(shots)] for k in range(CHUNK // 2)]

    def done(chunk, _):
        for_sides(sides_y, lambda side, index: y_copy(STEPS, chunk, side, index).wait_send())
        return 0

    lax.fori_loop(0, chunks, done, 0)
    for_sides(sides_x, lambda side, index: x_copy(STEPS, side, index).wait_send())

    others = pltpu.make_async_remote_copy(
        src_ref=OUTG.at[pl.ds(0, shots - 1)],
        dst_ref=INC.at[pl.ds(0, shots - 1)],
        send_sem=g_send,
        recv_sem=g_recv,
        device_id={"shot": lax.rem(me + 1, shots)},
        device_id_type=MESH,
    )
    others.wait_send()
    for copy in out_copies():
        copy.wait()
    others.wait_recv()
    for k in range(CHUNK // 2):
        total = None
        for shot in range(shots):
            term = weights[k][shot] * INC[shot]
            total = term if total is None else total + term
        grad_out[0, k] = total


def hand_on(fwd, adj, grad, fwd_out, adj_out, grad_out, fwd_here, adj_here, grad_here, sems):
    pieces = 4
    size = fwd.shape[1] // pieces
    ways = [(grad, grad_here, grad_out)]
    for src, here, dst in ((fwd, fwd_here, fwd_out), (adj, adj_here, adj_out)):
        for p in range(pieces):
            x = pl.ds(p * size, size)
            ways.append((src.at[:, x], here.at[:, x], dst.at[:, x]))
    ways = [
        (pltpu.make_async_copy(src, here, sems.at[0, i]), pltpu.make_async_copy(here, dst, sems.at[1, i]))
        for i, (src, here, dst) in enumerate(ways)
    ]
    for arrive, _ in ways:
        arrive.start()
    for arrive, leave in ways:
        arrive.wait()
        leave.start()
    for _, leave in ways:
        leave.wait()


def body(
    stiffness, buoyancy, fwd_prev, fwd_now, adj_prev, adj_now, wavelet, source_cell, receiver_cell,
    traces, aperture_blocks, aperture_count,
):
    nx, ny, nz = stiffness.shape
    shots = lax.axis_size("shot")
    nrec = traces.shape[1]
    chunks = nx // CHUNK
    xe, ye = nx + 2 * WIDTH, ny + 2 * TOP
    f32, bf16, i32 = jnp.float32, jnp.bfloat16, jnp.int32
    hbm = pl.BlockSpec(memory_space=pltpu.HBM)
    vmem = pl.BlockSpec(memory_space=pltpu.VMEM)
    dma = pltpu.SemaphoreType.DMA
    receivers = jnp.transpose(receiver_cell, (2, 0, 1))
    by_step = jnp.transpose(traces, (0, 2, 1))
    lists = jnp.swapaxes(aperture_blocks, 3, 4)
    out_shape = (
        jax.ShapeDtypeStruct(fwd_now.shape, f32),
        jax.ShapeDtypeStruct(adj_now.shape, f32),
        jax.ShapeDtypeStruct((1, nx // 2 // shots, ny // 2, nz // 2), f32),
    )
    results = pl.pallas_call(
        kernel,
        out_shape=out_shape,
        in_specs=[hbm] * 12,
        out_specs=(pl.BlockSpec(memory_space=pl.ANY),) * 2 + (vmem,),
        scratch_shapes=[
            pltpu.VMEM((2, xe, 2, ye, LANES), f32),
            pltpu.VMEM((3, xe, 2, ye, LANES), f32),
            pltpu.VMEM((2, xe, 2, ye, LANES), f32),
            pltpu.VMEM((2, xe, 2, ye, LANES), f32),
            pltpu.VMEM((2, xe, 2, ye, LANES), f32),
            pltpu.VMEM((2, xe, 2, ye, LANES), f32),
            pltpu.VMEM((nx, 2, ny, LANES), f32),
            pltpu.VMEM((4, nx, 2, ny, LANES), f32),
            pltpu.VMEM((STEPS, nx, 2, ny, LANES), f32),
            pltpu.VMEM((STEPS, nx, 2, ny, LANES), f32),
            pltpu.VMEM((nx * ny, nrec), bf16),
            pltpu.VMEM((STEPS, nz, nrec), bf16),
            pltpu.VMEM((STEPS, nz, nrec), bf16),
            pltpu.VMEM((nz, 2 * nz), bf16),
            pltpu.VMEM((nz, nz // 2), bf16),
            pltpu.VMEM((2, 2, nx, 2, ny, LANES), f32),
            pltpu.VMEM((2, 2, nx, 2, ny, LANES), f32),
            pltpu.VMEM((2, ny, LANES), f32),
            pltpu.VMEM((CHUNK // 2, 2, ny, LANES), f32),
            pltpu.VMEM((shots, ny // 2, nz // 2), f32),
            pltpu.VMEM((shots, ny // 2, nz // 2), f32),
            pltpu.VMEM(receivers.shape, i32),
            pltpu.VMEM(by_step.shape, f32),
            pltpu.SMEM(wavelet.shape, f32),
            pltpu.SMEM(source_cell.shape, i32),
            pltpu.SMEM((shots,) + lists.shape[3:], i32),
            pltpu.SMEM((shots,) + aperture_count.shape[2:], i32),
            dma((12,)),
            dma((2,)),
            dma((2, 2)),
            dma((chunks, 2)),
            dma((2, chunks, 2)),
            dma((2, 2)),
            dma(()),
            dma(()),
        ],
        compiler_params=pltpu.CompilerParams(
            collective_id=0, has_side_effects=True, vmem_limit_bytes=60 << 20
        ),
        name="window",
    )(
        stiffness, buoyancy, fwd_prev, fwd_now, adj_prev, adj_now, wavelet, source_cell,
        receivers, by_step, lists, aperture_count,
    )
    return pl.pallas_call(
        hand_on,
        out_shape=out_shape,
        in_specs=[hbm] * 3,
        out_specs=(hbm,) * 3,
        scratch_shapes=[pltpu.VMEM(out.shape, f32) for out in out_shape] + [dma((2, 9))],
        name="hand_on",
    )(*results)


def solution(mesh):
    in_specs = (
        P("gx", "gy", None),
        P("gx", "gy", None),
        P("shot", "gx", "gy", None),
        P("shot", "gx", "gy", None),
        P("shot", "gx", "gy", None),
        P("shot", "gx", "gy", None),
        P("shot", None),
        P("shot", None),
        P("shot", None, None),
        P("shot", None, None),
        P(),
        P(),
    )
    out_specs = (
        P("shot", "gx", "gy", None),
        P("shot", "gx", "gy", None),
        P("gx", "shot", "gy", None),
    )
    return jax.shard_map(body, mesh=mesh, in_specs=in_specs, out_specs=out_specs, check_vma=False)
```

```python
import jax
import jax.numpy as jnp
from jax import lax
from jax.experimental import pallas as pl
from jax.experimental.pallas import tpu as pltpu
from jax.sharding import PartitionSpec as P

MESH = pl.DeviceIdType.MESH
STEPS = 4
WIDTH = 4
BLOCK = 48
CHUNK = 6
TOP = 8
LANES = 128

C1, D1 = 8.0 / 5.0, 4.0 / 5.0
second = tuple(c / C1 for c in (-205.0 / 72.0, 8.0 / 5.0, -1.0 / 5.0, 8.0 / 315.0, -1.0 / 560.0))
first = tuple(d / D1 for d in (4.0 / 5.0, -1.0 / 5.0, 4.0 / 105.0, -1.0 / 280.0))


def split(v):
    high = v.astype(jnp.bfloat16)
    return high, (v - high.astype(jnp.float32)).astype(jnp.bfloat16)


def dot(a, b):
    return jnp.dot(a, b, preferred_element_type=jnp.float32)


def dot_nt(a, b):
    return lax.dot_general(a, b, (((1,), (1,)), ((), ())), preferred_element_type=jnp.float32)


def kernel(
    stiff, buoy, fwd0, fwd1, adj0, adj1, wave_in, source_in, receiver_in, traces_in, blocks_in, counts_in,
    fwd_out, adj_out, grad_out,
    F0, F1, F2, F3, F4, F5, K, CO, R, Q, A, BH, BL, CZ, PZ, Z0, Z1, SM, TI, OUTG, INC,
    receiver, traces, wave, source, blocks, counts,
    load_sem, x_send, x_recv, y_send, y_recv, out_sem, g_send, g_recv,
):
    levels = (F0, F1, F2, F3, F4, F5)
    depth = (Z0, Z1)
    B = F1.at[2]
    nx, ny, nz = stiff.shape
    chunks = nx // CHUNK
    gx, gy, me = lax.axis_index("gx"), lax.axis_index("gy"), lax.axis_index("shot")
    last_x, last_y = lax.axis_size("gx") - 1, lax.axis_size("gy") - 1
    shots = lax.axis_size("shot")
    own = pl.ds(TOP, ny)
    inner = pl.ds(WIDTH, nx)
    sides_x = ((gx > 0, gx - 1), (gx < last_x, gx + 1))
    sides_y = ((gy > 0, gy - 1), (gy < last_y, gy + 1))

    def for_sides(sides, do):
        for side, (there, index) in enumerate(sides):
            @pl.when(there)
            def _():
                do(side, index)

    barrier = pltpu.get_barrier_semaphore()
    peers = shots - 1
    for axis, sides in (("gx", sides_x), ("gy", sides_y)):
        for there, index in sides:
            @pl.when(there)
            def _():
                pl.semaphore_signal(barrier, inc=1, device_id={axis: index}, device_id_type=MESH)
            peers = peers + jnp.where(there, 1, 0)

    def greet(step, _):
        pl.semaphore_signal(
            barrier, inc=1, device_id={"shot": lax.rem(me + step, shots)}, device_id_type=MESH
        )
        return 0

    lax.fori_loop(1, shots, greet, 0)

    small = [
        pltpu.make_async_copy(src, dst, load_sem.at[6 + i])
        for i, (src, dst) in enumerate(
            (
                (receiver_in, receiver),
                (traces_in, traces),
                (wave_in, wave),
                (source_in, source),
                (blocks_in.at[:, gx, gy], blocks),
                (counts_in.at[:, gx], counts),
            )
        )
    ]
    large = (
        (buoy, F1.at[2, inner, :, own, :]),
        (fwd1.at[0], F1.at[0, inner, :, own, :]),
        (adj1.at[0], F1.at[1, inner, :, own, :]),
        (stiff, K),
        (fwd0.at[0], F0.at[0, inner, :, own, :]),
        (adj0.at[0], F0.at[1, inner, :, own, :]),
    )

    def load(i):
        src, dst = large[i]
        for half in range(2):
            pltpu.make_async_copy(
                src.at[:, :, pl.ds(half * LANES, LANES)], dst.at[:, half], load_sem.at[i]
            ).start()

    def loaded(i):
        dst = large[i][1]
        pltpu.make_async_copy(dst, dst, load_sem.at[i]).wait()

    for copy in small[:4]:
        copy.start()
    for i in range(6):
        load(i)
    for copy in small[4:]:
        copy.start()

    for side, (there, _) in enumerate(sides_x):
        @pl.when(jnp.logical_not(there))
        def _():
            at = pl.ds(side * (nx + WIDTH), WIDTH)
            for ref in levels[1 : STEPS + 1]:
                for field in range(ref.shape[0]):
                    ref[field, at, :, own, :] = jnp.zeros((WIDTH, 2, ny, LANES), jnp.float32)
    for side, (there, _) in enumerate(sides_y):
        @pl.when(jnp.logical_not(there))
        def _():
            at = pl.ds(TOP - WIDTH + side * (ny + WIDTH), WIDTH)

            def clear(x, _):
                for ref in levels[1 : STEPS + 1]:
                    for field in range(ref.shape[0]):
                        ref[field, x, :, at, :] = jnp.zeros((2, WIDTH, LANES), jnp.float32)
                return 0

            lax.fori_loop(WIDTH, nx + WIDTH, clear, 0)

    def x_edge(side):
        return pl.ds(WIDTH + side * (nx - WIDTH), WIDTH), pl.ds((1 - side) * (nx + WIDTH), WIDTH)

    def y_edge(side):
        return (
            pl.ds(TOP + side * (ny - WIDTH), WIDTH),
            pl.ds(TOP - WIDTH + (1 - side) * (ny + WIDTH), WIDTH),
        )

    def x_copy(level, side, index, arrival=False):
        ref = levels[level]
        mine, theirs = x_edge(1 - side if arrival else side)
        return pltpu.make_async_remote_copy(
            src_ref=ref.at[:, theirs if arrival else mine, :, own, :],
            dst_ref=ref.at[:, theirs, :, own, :],
            send_sem=x_send.at[side],
            recv_sem=x_recv.at[level % 2, side if arrival else 1 - side],
            device_id={"gx": index},
            device_id_type=MESH,
        )

    def y_copy(level, chunk, side, index, arrival=False):
        ref = levels[level]
        mine, theirs = y_edge(1 - side if arrival else side)
        x = pl.ds(WIDTH + chunk * CHUNK, CHUNK)
        return pltpu.make_async_remote_copy(
            src_ref=ref.at[:, x, :, theirs if arrival else mine, :],
            dst_ref=ref.at[:, x, :, theirs, :],
            send_sem=y_send.at[chunk, side],
            recv_sem=y_recv.at[level % 2, chunk, side if arrival else 1 - side],
            device_id={"gy": index},
            device_id_type=MESH,
        )

    def order(i):
        return lax.rem(chunks - i, chunks)

    def on_border(chunk, do):
        for side, border in enumerate((0, chunks - 1)):
            there, index = sides_x[side]

            @pl.when((chunk == border) & there)
            def _():
                do(side, index)

    def await_halos(level, chunk):
        on_border(chunk, lambda side, index: x_copy(level, side, index, True).wait_recv())
        for_sides(sides_y, lambda side, index: y_copy(level, chunk, side, index, True).wait_recv())

    for i in range(3):
        loaded(i)
    pl.semaphore_wait(barrier, peers)
    for_sides(sides_x, lambda side, index: x_copy(1, side, index).start())

    def first_strips(i, _):
        for_sides(sides_y, lambda side, index: y_copy(1, order(i), side, index).start())
        return 0

    lax.fori_loop(0, chunks, first_strips, 0)

    diff = lax.broadcasted_iota(jnp.int32, (nz, nz), 0) - lax.broadcasted_iota(jnp.int32, (nz, nz), 1)
    lap = jnp.zeros((nz, nz), jnp.float32)
    der = jnp.zeros((nz, nz), jnp.float32)
    for reach in range(1, WIDTH + 1):
        lap = jnp.where(jnp.abs(diff) == reach, second[reach], lap)
        der = jnp.where(diff == reach, first[reach - 1], der)
        der = jnp.where(diff == -reach, -first[reach - 1], der)
    CZ[:, 0:nz] = lap.astype(jnp.bfloat16)
    CZ[:, nz:] = der.astype(jnp.bfloat16)
    fine = lax.broadcasted_iota(jnp.int32, (nz, nz // 2), 0)
    pair = lax.broadcasted_iota(jnp.int32, (nz, nz // 2), 1) * 2
    PZ[...] = jnp.where((fine == pair) | (fine == pair + 1), 0.125, 0.0).astype(jnp.bfloat16)

    for copy in small[:4]:
        copy.wait()

    for half in range(2):
        row = lax.broadcasted_iota(jnp.int32, (ny, LANES), 0) + gy * ny
        col = lax.broadcasted_iota(jnp.int32, (ny, LANES), 1) + half * LANES
        SM[half] = jnp.where((row == source[0, 1]) & (col == source[0, 2]), 1.0, 0.0)

    rec_x = receiver[0] - gx * nx
    rec_y = receiver[1] - gy * ny
    inside = (rec_x >= 0) & (rec_x < nx) & (rec_y >= 0) & (rec_y < ny)
    cell = jnp.where(inside, rec_x * ny + rec_y, -1)
    nrec = cell.shape[1]
    rows = 128

    def hot(g, _):
        at = lax.broadcasted_iota(jnp.int32, (rows, nrec), 0) + g * rows
        A[pl.ds(pl.multiple_of(g * rows, rows), rows), :] = jnp.where(at == cell, 1.0, 0.0).astype(
            jnp.bfloat16
        )
        return 0

    lax.fori_loop(0, nx * ny // rows, hot, 0)
    rec_z = receiver[2]
    for n in range(STEPS):
        def place(g, _):
            at = lax.broadcasted_iota(jnp.int32, (64, nrec), 0) + g * 64
            high, low = split(jnp.where(at == rec_z, traces[0, n : n + 1, :], 0.0))
            where = pl.ds(pl.multiple_of(g * 64, 64), 64)
            BH[n, where, :] = high
            BL[n, where, :] = low
            return 0

        lax.fori_loop(0, nz // 64, place, 0)

    def inject(n, _):
        for part in range(2):
            hots = A[pl.ds(part * nx * ny // 2, nx * ny // 2), :]
            field = dot_nt(hots, BH[n]) + dot_nt(hots, BL[n])
            field = field.reshape(nx // 2, ny, nz)
            for half in range(2):
                R[n, pl.ds(part * nx // 2, nx // 2), half] = field[:, :, half * LANES : (half + 1) * LANES]
        return 0

    lax.fori_loop(0, STEPS, inject, 0)

    def along_depth(ref, block, out_ref):
        x = pl.ds(WIDTH + block * BLOCK, BLOCK)
        cells = BLOCK * ny
        parts = [
            jnp.concatenate(
                [ref[field, x, half, own, :].reshape(cells, LANES) for half in range(2)], axis=1
            )
            for field in range(2)
        ]
        high, low = split(jnp.concatenate(parts, axis=0))
        out = dot(high, CZ[...]) + dot(low, CZ[...])
        for field in range(2):
            for kind in range(2):
                for half in range(2):
                    at = kind * nz + half * LANES
                    piece = out[field * cells : (field + 1) * cells, at : at + LANES]
                    out_ref[field, kind, pl.ds(block * BLOCK, BLOCK), half] = piece.reshape(
                        BLOCK, ny, LANES
                    )

    def slopes(along, x, half):
        total = None
        for reach in range(1, WIDTH + 1):
            if along == 0:
                ahead, behind = B[x + reach, half, own, :], B[x - reach, half, own, :]
            else:
                ahead = B[x, half, pl.ds(TOP + reach, ny), :]
                behind = B[x, half, pl.ds(TOP - reach, ny), :]
            term = ahead - behind
            if reach > 1:
                term = first[reach - 1] * term
            total = term if total is None else total + term
        return total

    loaded(3)

    def prepare(block, _):
        x = pl.ds(WIDTH + block * BLOCK, BLOCK)
        xk = pl.ds(block * BLOCK, BLOCK)
        parts = [B[x, half, own, :].reshape(BLOCK * ny, LANES) for half in range(2)]
        high, low = split(jnp.concatenate(parts, axis=1))
        der_z = dot(high, CZ[:, nz:]) + dot(low, CZ[:, nz:])
        for half in range(2):
            stiffness = K[xk, half]
            CO[0, xk, half] = C1 * stiffness * parts[half].reshape(BLOCK, ny, LANES)
            along = der_z[:, half * LANES : (half + 1) * LANES].reshape(BLOCK, ny, LANES)
            CO[4, xk, half] = 2.0 + (3.0 * second[0]) * CO[0, xk, half]
            CO[3, xk, half] = (D1 * D1) * stiffness * along
        return 0

    lax.fori_loop(0, nx // BLOCK, prepare, 0)

    def all_depths(level):
        def one(block, _):
            along_depth(levels[level], block, depth[(level + 1) % 2])
            return 0

        lax.fori_loop(0, nx // BLOCK, one, 0)

    all_depths(1)

    def coefficients(chunk):
        def plane(j, _):
            x = chunk * CHUNK + j
            for half in range(2):
                stiffness = (D1 * D1) * K[x, half]
                CO[1, x, half] = stiffness * slopes(0, WIDTH + x, half)
                CO[2, x, half] = stiffness * slopes(1, WIDTH + x, half)
            return 0

        lax.fori_loop(0, CHUNK, plane, 0)

    for i in (4, 5):
        loaded(i)

    def stencil(n, chunk, half):
        before, now, after = levels[n], levels[n + 1], levels[n + 2]
        x0 = chunk * CHUNK
        amplitudes = [
            jnp.where(source[0, 0] - gx * nx == x0 + j, wave[0, n], 0.0) for j in range(CHUNK)
        ]
        for top in range(0, ny, 8):
            tile = pl.ds(TOP + top, 8)
            row = pl.ds(top, 8)
            planes = [
                [now[field, x0 + k, half, tile, :] for k in range(CHUNK + 2 * WIDTH)]
                for field in range(2)
            ]
            for j in range(CHUNK):
                x = x0 + j
                co = [CO[i, x, half, row, :] for i in range(4)]
                for field in range(2):
                    xs = planes[field]
                    here = xs[WIDTH + j]
                    lap = depth[n % 2][field, 0, x, half, row, :]
                    if field == 0:
                        lap = (3.0 * second[0]) * here + lap
                    der_x = der_y = None
                    for reach in range(1, WIDTH + 1):
                        xa, xb = xs[WIDTH + j + reach], xs[WIDTH + j - reach]
                        ya = now[field, x + WIDTH, half, pl.ds(TOP + top + reach, 8), :]
                        yb = now[field, x + WIDTH, half, pl.ds(TOP + top - reach, 8), :]
                        pairs = (xa + xb) + (ya + yb)
                        dx, dy = xa - xb, ya - yb
                        if reach == 1:
                            lap, der_x, der_y = lap + pairs, dx, dy
                        else:
                            lap = lap + second[reach] * pairs
                            der_x = der_x + first[reach - 1] * dx
                            der_y = der_y + first[reach - 1] * dy
                    change = co[0] * lap + co[1] * der_x + co[2] * der_y
                    change = change + co[3] * depth[n % 2][field, 1, x, half, row, :]
                    if field == 0:
                        change = change + amplitudes[j] * SM[half, row, :]
                        Q[n, x, half, row, :] = change
                    else:
                        change = change + R[n, x, half, row, :]
                    old = before[field, x + WIDTH, half, tile, :]
                    after[field, x + WIDTH, half, tile, :] = (
                        (2.0 if field == 0 else CO[4, x, half, row, :]) * here - old
                    ) + change

    def send_on(level, chunk):
        def face(side, index):
            x_copy(level - 1, side, index).wait_send()
            x_copy(level, side, index).start()

        def strip(side, index):
            y_copy(level - 1, chunk, side, index).wait_send()
            y_copy(level, chunk, side, index).start()

        on_border(chunk, face)
        for_sides(sides_y, strip)

    def out_copies():
        for field, out in enumerate((fwd_out, adj_out)):
            for half in range(2):
                yield pltpu.make_async_copy(
                    F5.at[field, inner, half, own, :],
                    out.at[0, :, :, pl.ds(half * LANES, LANES)],
                    out_sem.at[field, half],
                )

    def chosen(shot, owner, k):
        valid = (blocks[shot, 0, owner] == k) & (counts[shot, gy, owner] > 0)
        return jnp.where(valid, 1.0, 0.0)

    def imaging(chunk):
        x0 = chunk * CHUNK
        for k in range(CHUNK // 2):
            for half in range(2):
                total = None
                for odd in range(2):
                    x = x0 + 2 * k + odd
                    for later in range(2, STEPS + 2):
                        term = levels[later][1, x + WIDTH, half, own, :] * Q[STEPS + 1 - later, x, half]
                        total = term if total is None else total + term
                TI[k, half] = total
        rows_k = []
        for k in range(CHUNK // 2):
            halves = [
                TI[k, half, pl.ds(0, ny // 2, stride=2), :] + TI[k, half, pl.ds(1, ny // 2, stride=2), :]
                for half in range(2)
            ]
            rows_k.append(jnp.concatenate(halves, axis=1))
        high, low = split(jnp.concatenate(rows_k, axis=0))
        coarse = dot(high, PZ[...]) + dot(low, PZ[...])
        row = None
        for k in range(CHUNK // 2):
            term = chosen(me, chunk, k) * coarse[k * (ny // 2) : (k + 1) * (ny // 2), :]
            row = term if row is None else row + term
        return row

    def deliver(chunk, row):
        @pl.when(chunk == me)
        def _():
            INC[me] = row

        @pl.when(chunk != me)
        def _():
            OUTG[chunk] = row
            pltpu.make_async_remote_copy(
                src_ref=OUTG.at[chunk],
                dst_ref=INC.at[me],
                send_sem=g_send,
                recv_sem=g_recv,
                device_id={"shot": chunk},
                device_id_type=MESH,
            ).start()

    for copy in small[4:]:
        copy.wait()

    for n in range(STEPS):
        def run(i, _):
            chunk = order(i)
            await_halos(n + 1, chunk)
            if n == 0:
                coefficients(chunk)
            if n == STEPS - 1:
                earlier = order(lax.rem(i + chunks - 1, chunks))
                row = imaging(earlier)
            for half in range(2):
                stencil(n, chunk, half)
            if n < STEPS - 1:
                send_on(n + 2, chunk)
            else:
                @pl.when(i > 0)
                def _():
                    deliver(earlier, row)
            return 0

        lax.fori_loop(0, chunks, run, 0)
        if n < STEPS - 1:
            all_depths(n + 2)
        else:
            deliver(order(chunks - 1), imaging(order(chunks - 1)))

    for copy in out_copies():
        copy.start()
    weights = [[chosen(shot, me, k) for shot in range(shots)] for k in range(CHUNK // 2)]

    def done(chunk, _):
        for_sides(sides_y, lambda side, index: y_copy(STEPS, chunk, side, index).wait_send())
        return 0

    lax.fori_loop(0, chunks, done, 0)
    for_sides(sides_x, lambda side, index: x_copy(STEPS, side, index).wait_send())

    others = pltpu.make_async_remote_copy(
        src_ref=OUTG.at[pl.ds(0, shots - 1)],
        dst_ref=INC.at[pl.ds(0, shots - 1)],
        send_sem=g_send,
        recv_sem=g_recv,
        device_id={"shot": lax.rem(me + 1, shots)},
        device_id_type=MESH,
    )
    others.wait_send()
    for copy in out_copies():
        copy.wait()
    others.wait_recv()
    for k in range(CHUNK // 2):
        total = None
        for shot in range(shots):
            term = weights[k][shot] * INC[shot]
            total = term if total is None else total + term
        grad_out[0, k] = total


def hand_on(fwd, adj, grad, fwd_out, adj_out, grad_out, fwd_here, adj_here, grad_here, sems):
    pieces = 4
    size = fwd.shape[1] // pieces
    ways = [(grad, grad_here, grad_out)]
    for src, here, dst in ((fwd, fwd_here, fwd_out), (adj, adj_here, adj_out)):
        for p in range(pieces):
            x = pl.ds(p * size, size)
            ways.append((src.at[:, x], here.at[:, x], dst.at[:, x]))
    ways = [
        (pltpu.make_async_copy(src, here, sems.at[0, i]), pltpu.make_async_copy(here, dst, sems.at[1, i]))
        for i, (src, here, dst) in enumerate(ways)
    ]
    for arrive, _ in ways:
        arrive.start()
    for arrive, leave in ways:
        arrive.wait()
        leave.start()
    for _, leave in ways:
        leave.wait()


def body(
    stiffness, buoyancy, fwd_prev, fwd_now, adj_prev, adj_now, wavelet, source_cell, receiver_cell,
    traces, aperture_blocks, aperture_count,
):
    nx, ny, nz = stiffness.shape
    shots = lax.axis_size("shot")
    nrec = traces.shape[1]
    chunks = nx // CHUNK
    xe, ye = nx + 2 * WIDTH, ny + 2 * TOP
    f32, bf16, i32 = jnp.float32, jnp.bfloat16, jnp.int32
    hbm = pl.BlockSpec(memory_space=pltpu.HBM)
    vmem = pl.BlockSpec(memory_space=pltpu.VMEM)
    dma = pltpu.SemaphoreType.DMA
    receivers = jnp.transpose(receiver_cell, (2, 0, 1))
    by_step = jnp.transpose(traces, (0, 2, 1))
    lists = jnp.swapaxes(aperture_blocks, 3, 4)
    out_shape = (
        jax.ShapeDtypeStruct(fwd_now.shape, f32),
        jax.ShapeDtypeStruct(adj_now.shape, f32),
        jax.ShapeDtypeStruct((1, nx // 2 // shots, ny // 2, nz // 2), f32),
    )
    results = pl.pallas_call(
        kernel,
        out_shape=out_shape,
        in_specs=[hbm] * 12,
        out_specs=(pl.BlockSpec(memory_space=pl.ANY),) * 2 + (vmem,),
        scratch_shapes=[
            pltpu.VMEM((2, xe, 2, ye, LANES), f32),
            pltpu.VMEM((3, xe, 2, ye, LANES), f32),
            pltpu.VMEM((2, xe, 2, ye, LANES), f32),
            pltpu.VMEM((2, xe, 2, ye, LANES), f32),
            pltpu.VMEM((2, xe, 2, ye, LANES), f32),
            pltpu.VMEM((2, xe, 2, ye, LANES), f32),
            pltpu.VMEM((nx, 2, ny, LANES), f32),
            pltpu.VMEM((5, nx, 2, ny, LANES), f32),
            pltpu.VMEM((STEPS, nx, 2, ny, LANES), f32),
            pltpu.VMEM((STEPS, nx, 2, ny, LANES), f32),
            pltpu.VMEM((nx * ny, nrec), bf16),
            pltpu.VMEM((STEPS, nz, nrec), bf16),
            pltpu.VMEM((STEPS, nz, nrec), bf16),
            pltpu.VMEM((nz, 2 * nz), bf16),
            pltpu.VMEM((nz, nz // 2), bf16),
            pltpu.VMEM((2, 2, nx, 2, ny, LANES), f32),
            pltpu.VMEM((2, 2, nx, 2, ny, LANES), f32),
            pltpu.VMEM((2, ny, LANES), f32),
            pltpu.VMEM((CHUNK // 2, 2, ny, LANES), f32),
            pltpu.VMEM((shots, ny // 2, nz // 2), f32),
            pltpu.VMEM((shots, ny // 2, nz // 2), f32),
            pltpu.VMEM(receivers.shape, i32),
            pltpu.VMEM(by_step.shape, f32),
            pltpu.SMEM(wavelet.shape, f32),
            pltpu.SMEM(source_cell.shape, i32),
            pltpu.SMEM((shots,) + lists.shape[3:], i32),
            pltpu.SMEM((shots,) + aperture_count.shape[2:], i32),
            dma((12,)),
            dma((2,)),
            dma((2, 2)),
            dma((chunks, 2)),
            dma((2, chunks, 2)),
            dma((2, 2)),
            dma(()),
            dma(()),
        ],
        compiler_params=pltpu.CompilerParams(
            collective_id=0, has_side_effects=True, vmem_limit_bytes=60 << 20
        ),
        name="window",
    )(
        stiffness, buoyancy, fwd_prev, fwd_now, adj_prev, adj_now, wavelet, source_cell,
        receivers, by_step, lists, aperture_count,
    )
    return pl.pallas_call(
        hand_on,
        out_shape=out_shape,
        in_specs=[hbm] * 3,
        out_specs=(hbm,) * 3,
        scratch_shapes=[pltpu.VMEM(out.shape, f32) for out in out_shape] + [dma((2, 9))],
        name="hand_on",
    )(*results)


def solution(mesh):
    in_specs = (
        P("gx", "gy", None),
        P("gx", "gy", None),
        P("shot", "gx", "gy", None),
        P("shot", "gx", "gy", None),
        P("shot", "gx", "gy", None),
        P("shot", "gx", "gy", None),
        P("shot", None),
        P("shot", None),
        P("shot", None, None),
        P("shot", None, None),
        P(),
        P(),
    )
    out_specs = (
        P("shot", "gx", "gy", None),
        P("shot", "gx", "gy", None),
        P("gx", "shot", "gy", None),
    )
    return jax.shard_map(body, mesh=mesh, in_specs=in_specs, out_specs=out_specs, check_vma=False)
```
